32 devices in a mesh: grp: 2 (over y), row: 4 (over z), col: 2 (over x), sub: 2 (over core).
Axes of the slice: x: 2, y: 2, z: 4, core: 2. Of those that a mesh axis runs over, the one named last changes fastest.
Arguments:
- recordings: float32 [4, 4096, 2000], P('grp', ('row', 'col'), 'sub'), parts along dimension 0, may hold values from -640 to 640
- filter_taps: float32 [129], replicated, may hold values from -0.5 to 0.5
- slot_table: int32 [4, 1024], P('row'), may hold values from 0 to 1023, each once within a row
- lag_count: int32 [4096], replicated, may hold values from 1 to 17
Outputs:
- xcorr: bfloat16 [34, 4096, 2, 2048], P('grp', ('row', 'sub'), 'col'), parts along dimension 0
The draws below stay inside these ranges and needn't reach their ends.
There are 2 independent parts, one for each index of `grp`. The reference program is written for one: setup_inputs(seed, part) draws one part's arguments, and reference() takes and returns one part's arrays. A program takes and returns all parts, laid end to end along the dimension named above; an argument that names none is the same for every part. Nothing has to cross between parts.
Inputs may be any that keep to these rules, and one draw needn't show every extreme that they name: Each row of slot_table names every slot of the block exactly once.
All inputs are finite; a program needn't handle non-finite values.
Results may differ from the reference program's by a relative error of at most 0.0052.
Values may be sent and summed in bfloat16 or wider, within the bound.
A program may use at most 192 MiB of HBM per device.

```python
import math
import jax
import jax.numpy as jnp
from jax import lax

C = 4096
SEGS = 2
TAPS = 129
LAGS = 17
TIME = 2000
TD = 1000
BLOCK = 1024
SPAN = 512
N_ROW = 4
N_COL = 2


def draw_recordings(key, part):
    key_scale, key_noise = jax.random.split(key, 2)
    channel_scale = jnp.exp(jax.random.uniform(key_scale, (SEGS, C, 1), jnp.float32, 0.0, math.log(10.0)))
    position = jnp.arange(TIME, dtype=jnp.float32) / TIME
    envelope = jnp.exp(position * math.log(10.0))
    base = jnp.clip(jax.random.normal(key_noise, (SEGS, C, TIME), jnp.float32), -4.0, 4.0)
    return (channel_scale * envelope * base).astype(jnp.float32)


def with_ends(drawn, rng, least, largest):
    longest = drawn.shape.index(max(drawn.shape))
    spots = []
    for shift in (0, 1):
        where = [jax.random.randint(jax.random.fold_in(rng, axis), (), 0, length) for axis, length in enumerate(drawn.shape)]
        where[longest] = (where[longest] + shift) % drawn.shape[longest]
        spots.append(tuple(where))
    return drawn.at[spots[0]].set(least).at[spots[1]].set(largest)


def scatter_about(rng, dims, spread, reach, held_as=jnp.bfloat16):
    return jnp.clip(spread * jax.random.normal(rng, dims, jnp.float32), -reach, reach).astype(held_as)


def setup_inputs(seed: int = 0, part: int = 0) -> dict:
    splits = jax.random.split(jax.random.key(seed), 5)
    own_keys = jax.random.split(jax.random.fold_in(splits[4], part), 5)
    recordings = draw_recordings(jax.random.fold_in(jax.random.fold_in(splits[4], part), 71), part)
    filter_taps = scatter_about(splits[1], (TAPS,), TAPS ** -0.5, 0.5, jnp.float32)
    slot_table = jax.vmap(lambda own: jax.random.permutation(own, BLOCK))(jax.random.split(splits[2], N_ROW)).reshape((N_ROW, BLOCK)).astype(jnp.int32)
    lag_count = with_ends(jax.random.randint(splits[3], (C,), 1, LAGS + 1), jax.random.fold_in(splits[3], 1), 1, LAGS).astype(jnp.int32)
    return {"recordings": recordings, "filter_taps": filter_taps, "slot_table": slot_table, "lag_count": lag_count}


stability = 1e-05

def reference(recordings, filter_taps, slot_table, lag_count):
    margin = (TAPS - 1) // 2
    padded = jnp.pad(recordings, ((0, 0), (0, 0), (margin, margin)))
    extent = padded.shape[2]
    filtered = lax.conv_general_dilated(padded.reshape(SEGS * C, 1, extent), filter_taps.reshape(1, 1, TAPS), (2,), 'VALID', precision=lax.Precision.HIGHEST).reshape(SEGS, C, TD)
    energy = lax.optimization_barrier(jnp.mean(filtered * filtered, axis=2, keepdims=True))
    whitened = (filtered * lax.rsqrt(energy + stability)).astype(jnp.bfloat16)
    chosen = (jnp.arange(N_ROW, dtype=jnp.int32)[:, None] * BLOCK + slot_table.astype(jnp.int32)).reshape(C)
    row_data = jnp.take(whitened, chosen, axis=1).astype(jnp.float32)
    column_data = whitened.reshape(SEGS, N_ROW, N_COL, SPAN, TD).transpose(0, 2, 1, 3, 4).reshape(SEGS, N_COL, N_ROW * SPAN, TD).astype(jnp.float32)
    lag_limits = lag_count.reshape(N_ROW, N_COL, SPAN).transpose(1, 0, 2).reshape(N_COL, N_ROW * SPAN)
    padded_cols = jnp.pad(column_data, ((0, 0), (0, 0), (0, 0), (0, LAGS)))
    factor = 1.0 / math.sqrt(SEGS * TD)

    def single_lag(lag_index):
        shifted = lax.dynamic_slice_in_dim(padded_cols, lag_index, TD, 3)
        product = jnp.einsum('sat,sqrt->aqr', row_data, shifted, precision=lax.Precision.HIGHEST)
        return jnp.where(lag_index < lag_limits[None], product * factor, 0.0).astype(jnp.bfloat16)
    return lax.map(single_lag, jnp.arange(LAGS, dtype=jnp.int32))
```

```python
import functools
import math

import jax
import jax.numpy as jnp
from jax import lax
from jax.experimental import pallas as pl
from jax.experimental.pallas import tpu as pltpu
from jax.sharding import PartitionSpec as P

LAGS = 17
PHASES = 8
SLOTS = 128
STABILITY = 1e-05
MESH = pl.DeviceIdType.MESH
VMEM_LIMIT = 40 << 20


def nt_dot(a, b):
    return lax.dot_general(a, b, (((1,), (1,)), ((), ())), preferred_element_type=jnp.float32)


def nn_dot(a, b):
    return jnp.dot(a, b, preferred_element_type=jnp.float32)


def filter_kernel(samples, side_ref, own_ref, other_ref, taps_ref, out_ref, line, filtered):
    margin = 64
    width = own_ref.shape[1]
    window = 3 * 128
    order = lax.broadcasted_iota(jnp.int32, (128, window), 0)
    place = PHASES * (order % 16) + order // 16
    band = jnp.broadcast_to(taps_ref[...], (128, window))
    for bit in range(7):
        moved = pltpu.roll(band, 2 << bit, 1)
        band = jnp.where((place >> bit) & 1 == 1, moved, band)
    band_high = band.astype(jnp.bfloat16)
    band_low = (band - band_high.astype(jnp.float32)).astype(jnp.bfloat16)

    line[...] = jnp.zeros_like(line)

    @pl.when(side_ref[0] == 0)
    def _():
        line[margin : margin + width] = own_ref[0]
        line[margin + width : margin + 2 * width] = other_ref[0]

    @pl.when(side_ref[0] != 0)
    def _():
        line[margin : margin + width] = other_ref[0]
        line[margin + width : margin + 2 * width] = own_ref[0]

    tiles = SLOTS // 16
    row = lax.broadcasted_iota(jnp.int32, (128, 1), 0)
    energy = jnp.zeros((1, line.shape[1]), jnp.float32)
    for tile in range(tiles):
        part = line[256 * tile : 256 * tile + window]
        high = part.astype(jnp.bfloat16)
        low = (part - high.astype(jnp.float32)).astype(jnp.bfloat16)
        value = nn_dot(band_high, high) + (nn_dot(band_high, low) + nn_dot(band_low, high))
        index = PHASES * (16 * tile + row % 16) + row // 16
        value = jnp.where(index < samples, value, 0.0)
        energy = energy + jnp.sum(value * value, axis=0, keepdims=True)
        filtered[tile] = value
    scale = lax.rsqrt(energy / samples + STABILITY)
    for tile in range(tiles):
        value = (filtered[tile] * scale).astype(jnp.bfloat16)
        for phase in range(PHASES):
            out_ref[phase, 0, 16 * tile : 16 * tile + 16, :] = value[16 * phase : 16 * phase + 16]


def whiten(recordings, other, taps, side):
    segments, width, channels = recordings.shape
    half = channels // 2
    block = min(128, half)
    steps = half // block
    samples = width
    own_steps = steps
    if block % 128:
        recordings = lax.dynamic_slice_in_dim(recordings, side[0] * half, half, 2)
        own_steps = 0
    taps_row = jnp.pad(taps.reshape(1, -1), ((0, 0), (0, 384 - taps.shape[0])))
    out = pl.pallas_call(
        functools.partial(filter_kernel, samples),
        out_shape=jax.ShapeDtypeStruct((PHASES, segments, SLOTS, half), jnp.bfloat16),
        grid_spec=pltpu.PrefetchScalarGridSpec(
            num_scalar_prefetch=1,
            grid=(segments, steps),
            in_specs=[
                pl.BlockSpec((1, width, block), lambda s, c, side: (s, 0, side[0] * own_steps + c)),
                pl.BlockSpec((1, width, block), lambda s, c, side: (s, 0, c)),
                pl.BlockSpec((1, 384), lambda s, c, side: (0, 0)),
            ],
            out_specs=pl.BlockSpec((PHASES, 1, SLOTS, block), lambda s, c, side: (0, s, 0, c)),
            scratch_shapes=[
                pltpu.VMEM((256 * (SLOTS // 16 - 1) + 384, block), jnp.float32),
                pltpu.VMEM((SLOTS // 16, 128, block), jnp.float32),
            ],
        ),
        compiler_params=pltpu.CompilerParams(vmem_limit_bytes=16 << 20),
        name="whiten",
    )(side, recordings, other, taps_row)
    return out.reshape(PHASES * segments * SLOTS, half)


def row_blocks():
    blocks = [[(j, 1)] for j in range(PHASES)]

    def minus(a, b):
        return a + [(index, -sign) for index, sign in b]

    def outer(kind, k):
        even, odd, after = [(1 + 2 * k, 1)], [(2 + 2 * k, 1)], [(3 + 2 * k, 1)]
        return [minus(even, odd), odd, minus(after, odd)][kind]

    blocks += [outer(1, k) for k in range(PHASES + 3)]
    for first in (0, 2):
        for second in range(3):
            for k in range(5):
                even, odd = outer(first, 2 * k), outer(first, 2 * k + 1)
                if second == 0:
                    blocks.append(minus(even, odd))
                elif second == 1:
                    blocks.append(odd)
                else:
                    blocks.append(minus(outer(first, 2 * k + 2), odd))
    return blocks


def column_blocks():
    blocks = [[2 * k, 2 * k + 1] for k in range(4)]
    for first in (0, 1):
        for second in ([0], [0, 2], [2]):
            blocks += [[4 * k + first + b for b in second] for k in range(2)]
    return blocks


ROW_BLOCKS = PHASES + PHASES + 3 + 30
COLUMN_BLOCKS = 16


def rows_kernel(count, base_ref, slots_ref, *refs):
    pieces, out_ref, pick, shifted = refs[:count], refs[count], refs[count + 1], refs[count + 2]
    phase = pl.program_id(0)
    rows = slots_ref.shape[0]
    depth = pieces[0].shape[0]

    @pl.when(phase == 0)
    def _():
        first = 0
        for k, piece in enumerate(pieces):
            width = piece.shape[1]
            channel = lax.broadcasted_iota(jnp.int32, (rows, width), 1) + base_ref[k]
            chosen = (slots_ref[...] == channel).astype(jnp.float32).astype(jnp.bfloat16)
            pick[:, first : first + width] = chosen
            first += width

    total = None
    first = 0
    for piece in pieces:
        width = piece.shape[1]
        term = nt_dot(pick[:, first : first + width], piece[...])
        first += width
        total = term if total is None else total + term
    for carry in range(3):
        moved = total
        if carry:
            moved = jnp.concatenate(
                [
                    pltpu.roll(total[:, s : s + SLOTS], carry, 1)
                    for s in range(0, depth, SLOTS)
                ],
                axis=1,
            )
        shifted[(2 - carry) * PHASES + phase] = moved.astype(jnp.bfloat16)

    @pl.when(phase == PHASES - 1)
    def _():
        def block(terms):
            if len(terms) == 1:
                return shifted[terms[0][0]]
            value = None
            for index, sign in terms:
                part = shifted[index].astype(jnp.float32) * sign
                value = part if value is None else value + part
            return value.astype(jnp.bfloat16)

        for slot, terms in enumerate(row_blocks()):
            out_ref[:, slot * depth : (slot + 1) * depth] = block(terms)


def build_rows(slots, pieces, bases):
    rows = slots.shape[0]
    depth = pieces[0].shape[0] // PHASES
    return pl.pallas_call(
        functools.partial(rows_kernel, len(pieces)),
        out_shape=jax.ShapeDtypeStruct((rows, ROW_BLOCKS * depth), jnp.bfloat16),
        grid_spec=pltpu.PrefetchScalarGridSpec(
            num_scalar_prefetch=1,
            grid=(PHASES,),
            in_specs=[pl.BlockSpec((rows, 1), lambda j, base: (0, 0))]
            + [pl.BlockSpec((depth, p.shape[1]), lambda j, base: (j, 0)) for p in pieces],
            out_specs=pl.BlockSpec(
                (rows, ROW_BLOCKS * depth), lambda j, base: (0, 0), pipeline_mode=pl.Buffered(1)
            ),
            scratch_shapes=[
                pltpu.VMEM((rows, sum(p.shape[1] for p in pieces)), jnp.bfloat16),
                pltpu.VMEM((3 * PHASES, rows, depth), jnp.bfloat16),
            ],
        ),
        compiler_params=pltpu.CompilerParams(vmem_limit_bytes=36 << 20),
        name="rows",
    )(bases, slots, *pieces)


def correlate_kernel(factor, count, choices, depth, where_ref, rows_ref, limit_ref, *refs):
    pieces = refs[: count * choices]
    out_ref, held, sums, done = refs[-4:]
    step = pl.program_id(0)
    length = PHASES * depth
    width = held.shape[2]

    @pl.when(step == 0)
    def _():
        for choice in range(choices):

            @pl.when(where_ref[3] == choice)
            def _():
                copies = [
                    pltpu.make_async_copy(pieces[count * choice + k], held.at[k], done.at[k])
                    for k in range(count)
                ]
                for copy in copies:
                    copy.start()
                for copy in copies:
                    copy.wait()

        for k in range(count):
            for slot, phases in enumerate(column_blocks()):
                value = None
                for phase in phases:
                    part = held[k, phase * depth : (phase + 1) * depth].astype(jnp.float32)
                    value = part if value is None else value + part
                sums[k, slot * depth : (slot + 1) * depth] = value.astype(jnp.bfloat16)

    block = min(width, 256)
    for k in range(count):
        for first in range(0, width, block):
            spot = first
            if count > 1:
                spot = pl.multiple_of(where_ref[1 + k] * width + first, block)
            limit = limit_ref[:, pl.ds(spot, block)]

            def write(slot, lag, product, spot=spot, limit=limit):
                value = jnp.where(lag < limit, product, 0.0)
                out_ref[slot, :, pl.ds(spot, block)] = value.astype(jnp.bfloat16)

            @pl.when(step < 4)
            def _():
                quad = 3 - step

                def product(row_slot, column_slot, length):
                    start = pl.multiple_of(row_slot * depth, depth)
                    return factor * nn_dot(
                        rows_ref[:, pl.ds(start, length * depth)],
                        sums[
                            k,
                            column_slot * depth : (column_slot + length) * depth,
                            first : first + block,
                        ],
                    )

                shared = [product(PHASES + 2 * quad + half, 0, 4) for half in range(2)]
                for outer, near in ((0, 0), (1, 1)):

                    def inner(kind):
                        index = 3 * outer + kind
                        return product(2 * PHASES + 3 + 5 * index + quad, 4 + 2 * index, 2)

                    middle = inner(1)
                    for half in range(2):
                        slot = 3 - 2 * half - near
                        write(slot, 4 * step + slot, shared[half] + (middle + inner(2 * half)))

            @pl.when(step == 4)
            def _():
                rows = rows_ref[:, :length]
                write(0, LAGS - 1, factor * nn_dot(rows, held[k, :, first : first + block]))


def correlate(rows, pieces, limits, where, factor, buffer):
    choices, count = len(pieces), len(pieces[0])
    depth = rows.shape[1] // ROW_BLOCKS
    length = PHASES * depth
    portion = rows.shape[0]
    columns = limits.shape[1]
    run = pieces[0][0].shape[1]
    across = count * run
    pieces = [piece for group in pieces for piece in group]
    operands = [where, rows, limits, *pieces]
    in_specs = [
        pl.BlockSpec(rows.shape, lambda l, where: (0, 0), pipeline_mode=pl.Buffered(1)),
        pl.BlockSpec((1, across), lambda l, where: (0, where[0])),
    ] + [pl.BlockSpec(memory_space=pl.ANY) for _ in pieces]
    aliases = {}
    if buffer is not None:
        aliases = {len(operands): 0}
        operands.append(buffer)
        in_specs.append(pl.BlockSpec(memory_space=pl.ANY))
    work = LAGS * portion * across
    return pl.pallas_call(
        functools.partial(correlate_kernel, factor, count, choices, depth),
        out_shape=jax.ShapeDtypeStruct((LAGS, portion, columns), jnp.bfloat16),
        grid_spec=pltpu.PrefetchScalarGridSpec(
            num_scalar_prefetch=1,
            grid=(pl.cdiv(LAGS, 4),),
            in_specs=in_specs,
            out_specs=pl.BlockSpec((4, portion, across), lambda l, where: (l, 0, where[0])),
            scratch_shapes=[
                pltpu.VMEM((count, length, run), jnp.bfloat16),
                pltpu.VMEM((count, COLUMN_BLOCKS * depth, run), jnp.bfloat16),
                pltpu.SemaphoreType.DMA((count,)),
            ],
        ),
        input_output_aliases=aliases,
        compiler_params=pltpu.CompilerParams(vmem_limit_bytes=24 << 20),
        cost_estimate=pl.CostEstimate(
            flops=2 * work * length,
            bytes_accessed=2 * (work + rows.size + length * across),
            transcendentals=0,
        ),
        name="correlate",
    )(*operands)


def whiten_segment(samples, band_high, band_low, line, filtered, store):
    window = 3 * 128
    tiles = SLOTS // 16
    row = lax.broadcasted_iota(jnp.int32, (128, 1), 0)
    energy = jnp.zeros((1, line.shape[1]), jnp.float32)
    for tile in range(tiles):
        part = line[256 * tile : 256 * tile + window]
        high = part.astype(jnp.bfloat16)
        low = (part - high.astype(jnp.float32)).astype(jnp.bfloat16)
        value = nn_dot(band_high, high) + (nn_dot(band_high, low) + nn_dot(band_low, high))
        index = PHASES * (16 * tile + row % 16) + row // 16
        value = jnp.where(index < samples, value, 0.0)
        energy = energy + jnp.sum(value * value, axis=0, keepdims=True)
        filtered[tile] = value
    scale = lax.rsqrt(energy / samples + STABILITY)
    for tile in range(tiles):
        value = (filtered[tile] * scale).astype(jnp.bfloat16)
        for phase in range(PHASES):
            store(phase, tile, value[16 * phase : 16 * phase + 16])


def sum_columns(held, sums):
    depth = sums.shape[0] // COLUMN_BLOCKS
    for slot, phases in enumerate(column_blocks()):
        value = held(phases[0])
        if len(phases) > 1:
            value = (value.astype(jnp.float32) + held(phases[1]).astype(jnp.float32)).astype(
                jnp.bfloat16
            )
        sums[slot * depth : (slot + 1) * depth] = value


def four_lags(rows_ref, sums, quad, first, block, write):
    depth = sums.shape[0] // COLUMN_BLOCKS

    def product(row_slot, column_slot, length):
        start = row_slot * depth
        if not isinstance(start, int):
            start = pl.multiple_of(start, depth)
        return nn_dot(
            rows_ref[:, pl.ds(start, length * depth)],
            sums[column_slot * depth : (column_slot + length) * depth, first : first + block],
        )

    shared = [product(PHASES + 2 * quad + half, 0, 4) for half in range(2)]
    for outer in range(2):

        def inner(kind):
            index = 3 * outer + kind
            return product(2 * PHASES + 3 + 5 * index + quad, 4 + 2 * index, 2)

        middle = inner(1)
        for half in range(2):
            write(3 - 2 * half - outer, shared[half] + (middle + inner(2 * half)))


def correlate_piece(factor, rows_ref, held, limits, sums, stage, last, copies, between, ahead):
    width = sums.shape[1]
    depth = sums.shape[0] // COLUMN_BLOCKS
    block = 256
    sum_columns(held, sums)

    def masked(product, lag, first):
        value = jnp.where(lag < limits[:, first : first + block], factor * product, 0.0)
        return value.astype(jnp.bfloat16)

    def step(turn, slot):
        for first in range(0, width, block):

            def write(index, product):
                stage[slot, index, :, first : first + block] = masked(
                    product, 4 * turn + index, first
                )

            four_lags(rows_ref, sums, 3 - turn, first, block, write)

    for turn in range(4):
        slot = turn % 2
        if ahead or turn >= 2:
            copies(turn - 2).wait()
        step(turn, slot)
        copies(turn).start()
        between(turn)
    if ahead:
        copies(-3).wait()
    for first in range(0, width, block):
        total = None
        for phase in range(0, PHASES, 8):
            part = nn_dot(
                rows_ref[:, : PHASES * depth],
                jnp.concatenate([held(p)[:, first : first + block] for p in range(PHASES)], axis=0),
            )
            total = part if total is None else total + part
        last[:, first : first + block] = masked(total, LAGS - 1, first)
    copies(4).start()
    between(4)


def orders(spot):
    return [
        spot,
        spot - 1 + 2 * ((3 - spot) // 3),
        spot + 1 + (3 - spot) // 3 - 3 * (spot // 3),
        3 * (1 - spot // 2),
    ]


CHUNKS = 4
EARLY = 3


def front_kernel(
    samples, factor,
    raw, taps_ref, slots_ref, limit_ref,
    rows_ref, cols, early,
    line, filtered, other, band_taps, pick, shifted, sums, stage, last,
    own_sem, raw_send, raw_recv, mate_send, mate_recv, x_send, x_recv, xm_send, xm_recv,
    z_send, z_recv, out_sem, last_sem,
):
    spot = lax.axis_index("row")
    across = lax.axis_index("col")
    side = lax.axis_index("sub")
    half = line.shape[2]
    channels = 2 * half
    rows = rows_ref.shape[0]
    margin = 64
    width = raw.shape[1]
    mine = pl.ds(pl.multiple_of(side * half, half), half)
    theirs = pl.ds(pl.multiple_of((1 - side) * half, half), half)
    mate = {"sub": 1 - side}
    beside = {"col": 1 - across}
    segments = 2

    place = pl.ds(pl.multiple_of(margin + side * width, 8), width)
    own = [
        pltpu.make_async_copy(raw.at[s, :, mine], line.at[s, place], own_sem.at[s])
        for s in range(segments)
    ]
    for copy in own:
        copy.start()

    barrier = pltpu.get_barrier_semaphore()
    pl.semaphore_signal(barrier, inc=1, device_id=mate, device_id_type=MESH)
    pl.semaphore_signal(barrier, inc=1, device_id=beside, device_id_type=MESH)

    @pl.when(spot > 0)
    def _():
        pl.semaphore_signal(barrier, inc=1, device_id={"row": spot - 1}, device_id_type=MESH)

    @pl.when(spot < 3)
    def _():
        pl.semaphore_signal(barrier, inc=1, device_id={"row": spot + 1}, device_id_type=MESH)

    pl.semaphore_wait(barrier, 2 + (spot + 2) // 3 + (5 - spot) // 3)

    def remote(source, target, send, recv, device):
        return pltpu.make_async_remote_copy(
            src_ref=source, dst_ref=target, send_sem=send, recv_sem=recv,
            device_id=device, device_id_type=MESH,
        )

    exchange = [
        remote(raw.at[s, :, theirs], line.at[s, place], raw_send.at[s], raw_recv.at[s], mate)
        for s in range(segments)
    ]
    for copy in exchange:
        copy.start()

    def chunk(buffer, k, lanes):
        return buffer.at[pl.ds(4 * (k % 2), 4), k // 2, :, lanes]

    def to_mate(z, k, lanes=mine):
        spotted = chunk(cols.at[z], k, lanes)
        return remote(spotted, spotted, mate_send.at[z, k], mate_recv.at[z, k], mate)

    def to_beside(k):
        return remote(
            chunk(cols.at[spot], k, mine), chunk(other, k, mine), x_send.at[k], x_recv.at[k], beside
        )

    def beside_to_mate(k, lanes=mine):
        spotted = chunk(other, k, lanes)
        return remote(spotted, spotted, xm_send.at[k], xm_recv.at[k], mate)

    def along(z, k, way):
        spotted = chunk(cols.at[z], k, mine)
        return remote(
            spotted, spotted, z_send.at[way, z, k], z_recv.at[z, k],
            {"row": spot + (1 if way else -1)},
        )

    def poll(distance, k):
        @pl.when(spot >= distance)
        def _():
            z = spot - distance
            along(z, k, 1).wait_recv()
            if distance < 3:

                @pl.when(spot < 3)
                def _():
                    along(z, k, 1).start()

            to_mate(z, k).start()

        @pl.when(spot + distance <= 3)
        def _():
            z = spot + distance
            along(z, k, 0).wait_recv()
            if distance < 3:

                @pl.when(spot > 0)
                def _():
                    along(z, k, 0).start()

            to_mate(z, k).start()

    def settle(distance, k):
        @pl.when(spot >= distance)
        def _():
            z = spot - distance
            if distance < 3:

                @pl.when(spot < 3)
                def _():
                    along(z, k, 1).wait_send()

            to_mate(z, k).wait_send()

        @pl.when(spot + distance <= 3)
        def _():
            z = spot + distance
            if distance < 3:

                @pl.when(spot > 0)
                def _():
                    along(z, k, 0).wait_send()

            to_mate(z, k).wait_send()

    window = 3 * 128
    band_taps[...] = jnp.zeros_like(band_taps)
    band_taps[:, : taps_ref.shape[1]] = taps_ref[...]
    order = lax.broadcasted_iota(jnp.int32, (128, window), 0)
    shift = PHASES * (order % 16) + order // 16
    band = jnp.broadcast_to(band_taps[...], (128, window))
    for bit in range(7):
        moved = pltpu.roll(band, 2 << bit, 1)
        band = jnp.where((shift >> bit) & 1 == 1, moved, band)
    band_high = band.astype(jnp.bfloat16)
    band_low = (band - band_high.astype(jnp.float32)).astype(jnp.bfloat16)

    end = margin + 2 * width
    for s in range(segments):
        line[s, :margin] = jnp.zeros((margin, half), jnp.float32)
        line[s, end:] = jnp.zeros((line.shape[1] - end, half), jnp.float32)

    slots = slots_ref[:, pl.ds(pl.multiple_of(side * rows, rows), rows)].astype(jnp.float32)
    slots = jnp.broadcast_to(slots, (128, rows)).T
    lane = lax.broadcasted_iota(jnp.int32, (rows, 128), 1)
    for which in range(2):
        first = (across if which == 0 else 1 - across) * channels
        for start in range(0, channels, 128):
            channel = (lane + (first + start)).astype(jnp.float32)
            pick[:, which * channels + start : which * channels + start + 128] = (
                (slots == channel).astype(jnp.float32).astype(jnp.bfloat16)
            )

    for s in range(segments):
        own[s].wait()
        exchange[s].wait_recv()

        def store(phase, tile, value, s=s):
            cols[spot, phase, s, 16 * tile : 16 * tile + 16, mine] = value

        whiten_segment(samples, band_high, band_low, line.at[s], filtered, store)
        for k in (2 * s, 2 * s + 1):
            to_beside(k).start()

            @pl.when(spot > 0)
            def _():
                along(spot, k, 0).start()

            @pl.when(spot < 3)
            def _():
                along(spot, k, 1).start()

            to_mate(spot, k).start()

    depth = segments * SLOTS
    for k in range(CHUNKS):
        s = k // 2
        to_beside(k).wait_recv()
        beside_to_mate(k).start()
        to_mate(spot, k, theirs).wait_recv()
        beside_to_mate(k, theirs).wait_recv()
        for phase in range(4 * (k % 2), 4 * (k % 2) + 4):
            total = nt_dot(pick[:, :channels], cols[spot, phase, s]) + nt_dot(
                pick[:, channels:], other[phase, s]
            )
            for carry in range(3):
                moved = pltpu.roll(total, carry, 1) if carry else total
                shifted[(2 - carry) * PHASES + phase] = moved.astype(jnp.bfloat16)
        poll(1, k)
        if k % 2:

            def tile(index, _, s=s):
                at = pl.ds(pl.multiple_of(index * 16, 16), 16)

                def write(slot, value):
                    rows_ref[at, slot * depth + s * SLOTS : slot * depth + (s + 1) * SLOTS] = value

                packed = [shifted[i, at] for i in range(3 * PHASES)]
                plain = [p.astype(jnp.float32) for p in packed]

                def outer(kind, k):
                    even, odd, after = plain[1 + 2 * k], plain[2 + 2 * k], None
                    if kind == 0:
                        return even - odd
                    return plain[3 + 2 * k] - odd

                for j in range(PHASES):
                    write(j, packed[j])
                for j in range(PHASES + 3):
                    write(PHASES + j, packed[2 + 2 * j])
                for number, kind in enumerate((0, 2)):
                    terms = [outer(kind, j) for j in range(PHASES + 3)]
                    at_slot = 2 * PHASES + 3 + 15 * number
                    for j in range(5):
                        odd = terms[2 * j + 1]
                        write(at_slot + j, (terms[2 * j] - odd).astype(jnp.bfloat16))
                        write(at_slot + 5 + j, odd.astype(jnp.bfloat16))
                        write(at_slot + 10 + j, (terms[2 * j + 2] - odd).astype(jnp.bfloat16))
                return 0

            lax.fori_loop(0, rows // 16, tile, 0)

    order_of = orders(spot)
    polls = {
        (0, 1): [(2, 0)], (0, 3): [(2, 1)],
        (1, 1): [(2, 2)], (1, 3): [(2, 3)],
        (2, 0): [(3, 0)], (2, 2): [(3, 1)], (2, 4): [(3, 2), (3, 3)],
    }

    def copies_of(index):
        def copies(turn):
            if turn == 4 or turn == -3:
                at = index if turn == 4 else index - 1
                return pltpu.make_async_copy(last, early.at[at, LAGS - 1], last_sem)
            at = index if turn >= 0 else index - 1
            return pltpu.make_async_copy(
                stage.at[turn % 2], early.at[at, pl.ds(4 * (turn % 4), 4)], out_sem.at[turn % 2]
            )

        return copies

    for index in range(EARLY):
        z = order_of[index]
        if index:
            for k in range(CHUNKS):
                to_mate(z, k, theirs).wait_recv()

        def held(phase, z=z):
            return cols[z, phase].reshape(depth, channels)

        limits = limit_ref[:, pl.ds(pl.multiple_of(z * 2 * channels + across * channels, channels), channels)]

        def between(turn, index=index):
            for distance, k in polls.get((index, turn), []):
                poll(distance, k)

        correlate_piece(
            factor, rows_ref, held, limits, sums, stage, last, copies_of(index), between, index > 0
        )
    for turn in (2, 3, 4):
        copies_of(EARLY - 1)(turn).wait()
    for k in range(CHUNKS):
        for index in range(EARLY, 4):
            to_mate(order_of[index], k, theirs).wait_recv()

    for s in range(segments):
        exchange[s].wait_send()
    for k in range(CHUNKS):
        to_beside(k).wait_send()
        beside_to_mate(k).wait_send()
        to_mate(spot, k).wait_send()

        @pl.when(spot > 0)
        def _():
            along(spot, k, 0).wait_send()

        @pl.when(spot < 3)
        def _():
            along(spot, k, 1).wait_send()

        for distance in (1, 2, 3):
            settle(distance, k)


def front(by_time, taps, slots, counts, factor):
    segments, width, channels = by_time.shape
    half = channels // 2
    rows = slots.shape[1] // 2
    depth = segments * SLOTS
    dma = pltpu.SemaphoreType.DMA
    vmem = pl.BlockSpec(memory_space=pltpu.VMEM)
    hbm = pl.BlockSpec(memory_space=pl.ANY)
    return pl.pallas_call(
        functools.partial(front_kernel, width, factor),
        out_shape=[
            jax.ShapeDtypeStruct((rows, ROW_BLOCKS * depth), jnp.bfloat16),
            jax.ShapeDtypeStruct((4, PHASES, segments, SLOTS, channels), jnp.bfloat16),
            jax.ShapeDtypeStruct((EARLY, LAGS, rows, channels), jnp.bfloat16),
        ],
        in_specs=[hbm, vmem, vmem, vmem],
        out_specs=[vmem, vmem, hbm],
        scratch_shapes=[
            pltpu.VMEM((segments, 256 * (SLOTS // 16 - 1) + 384, half), jnp.float32),
            pltpu.VMEM((SLOTS // 16, 128, half), jnp.float32),
            pltpu.VMEM((PHASES, segments, SLOTS, channels), jnp.bfloat16),
            pltpu.VMEM((1, 384), jnp.float32),
            pltpu.VMEM((rows, 2 * channels), jnp.bfloat16),
            pltpu.VMEM((3 * PHASES, rows, SLOTS), jnp.bfloat16),
            pltpu.VMEM((COLUMN_BLOCKS * depth, channels), jnp.bfloat16),
            pltpu.VMEM((2, 4, rows, channels), jnp.bfloat16),
            pltpu.VMEM((rows, channels), jnp.bfloat16),
            dma((2,)), dma((2,)), dma((2,)), dma((4, CHUNKS)), dma((4, CHUNKS)),
            dma((CHUNKS,)), dma((CHUNKS,)), dma((CHUNKS,)), dma((CHUNKS,)),
            dma((2, 4, CHUNKS)), dma((4, CHUNKS)), dma((2,)), dma,
        ],
        compiler_params=pltpu.CompilerParams(
            vmem_limit_bytes=VMEM_LIMIT, collective_id=0, has_side_effects=True
        ),
        name="front",
    )(by_time, taps, slots, counts)


GROUP = 9


def back_kernel(
    factor, rows_ref, cols, early, limit_ref, out_ref, sums, stage, last, ring,
    out_sem, last_sem, in_sem, ring_sem,
):
    spot = lax.axis_index("row")
    across = lax.axis_index("col")
    channels = sums.shape[1]
    depth = sums.shape[0] // COLUMN_BLOCKS
    order_of = orders(spot)
    slabs = [(i, lag) for i in range(EARLY) for lag in range(LAGS)]
    groups = [slabs[i : i + GROUP] for i in range(0, len(slabs), GROUP)]
    depth_of_ring = ring.shape[0]

    def columns(z):
        return pl.ds(pl.multiple_of(z * channels, channels), channels)

    def take(g):
        return [
            pltpu.make_async_copy(
                early.at[i, lag], ring.at[g % depth_of_ring, n], in_sem.at[g % depth_of_ring, n]
            )
            for n, (i, lag) in enumerate(groups[g])
        ]

    def give(g):
        return [
            pltpu.make_async_copy(
                ring.at[g % depth_of_ring, n],
                out_ref.at[lag, :, columns(order_of[i])],
                ring_sem.at[g % depth_of_ring, n],
            )
            for n, (i, lag) in enumerate(groups[g])
        ]

    def start(copies):
        for copy in copies:
            copy.start()

    def wait(copies):
        for copy in copies:
            copy.wait()

    def pump(g):
        if g < len(groups):
            wait(take(g))
            start(give(g))
        ahead = g + depth_of_ring - 1
        if ahead < len(groups):
            if g >= 1:
                wait(give(g - 1))
            start(take(ahead))

    for g in range(depth_of_ring - 1):
        start(take(g))

    z = order_of[3]
    limits = limit_ref[:, pl.ds(pl.multiple_of(z * 2 * channels + across * channels, channels), channels)]

    def held(phase):
        return cols[z, phase].reshape(depth, channels)

    def copies(turn):
        if turn == 4:
            return pltpu.make_async_copy(last, out_ref.at[LAGS - 1, :, columns(z)], last_sem)
        return pltpu.make_async_copy(
            stage.at[turn % 2], out_ref.at[pl.ds(4 * turn, 4), :, columns(z)], out_sem.at[turn % 2]
        )

    def between(turn):
        pump(turn)

    correlate_piece(factor, rows_ref, held, limits, sums, stage, last, copies, between, False)
    for g in range(5, len(groups)):
        pump(g)
    for g in range(max(0, len(groups) - depth_of_ring), len(groups)):
        wait(give(g))
    for turn in (2, 3, 4):
        copies(turn).wait()


def back(rows, cols, early, counts, factor):
    portion = rows.shape[0]
    channels = cols.shape[4]
    depth = rows.shape[1] // ROW_BLOCKS
    dma = pltpu.SemaphoreType.DMA
    vmem = pl.BlockSpec(memory_space=pltpu.VMEM)
    hbm = pl.BlockSpec(memory_space=pl.ANY)
    ring = 3
    return pl.pallas_call(
        functools.partial(back_kernel, factor),
        out_shape=jax.ShapeDtypeStruct((LAGS, portion, 4 * channels), jnp.bfloat16),
        in_specs=[vmem, vmem, hbm, vmem],
        out_specs=hbm,
        scratch_shapes=[
            pltpu.VMEM((COLUMN_BLOCKS * depth, channels), jnp.bfloat16),
            pltpu.VMEM((2, 4, portion, channels), jnp.bfloat16),
            pltpu.VMEM((portion, channels), jnp.bfloat16),
            pltpu.VMEM((ring, GROUP, portion, channels), jnp.bfloat16),
            dma((2,)), dma, dma((ring, GROUP)), dma((ring, GROUP)),
        ],
        compiler_params=pltpu.CompilerParams(vmem_limit_bytes=VMEM_LIMIT),
        name="back",
    )(rows, cols, early, counts)


def swap(value, axis):
    return lax.ppermute(value, axis, [(0, 1), (1, 0)])


def shards(recordings, filter_taps, slot_table, lag_count):
    segments, channels, width = recordings.shape
    half = channels // 2
    row_count = lax.axis_size("row")
    col_count = lax.axis_size("col")
    portion = slot_table.shape[1] // 2
    factor = 1.0 / math.sqrt(segments * width)
    by_time = recordings.transpose(0, 2, 1)

    if half % 256 == 0 and col_count == 2 and row_count == 4 and portion == channels:
        counts = lag_count.reshape(1, -1)
        taps = filter_taps.reshape(1, -1)
        rows, cols, early = front(by_time, taps, slot_table, counts, factor)
        result = back(rows, cols, early, counts, factor)
        return result.reshape(LAGS, portion, 1, -1)

    side = lax.axis_index("sub")
    across = lax.axis_index("col")
    away = lax.dynamic_slice_in_dim(by_time, (1 - side) * half, half, 2)
    other = swap(away, "sub")
    mine = whiten(by_time, other, filter_taps, side.reshape(1))
    slots = lax.dynamic_slice_in_dim(slot_table[0], side * portion, portion).reshape(portion, 1)
    limits = lax.dynamic_slice_in_dim(
        lag_count.reshape(row_count, col_count, channels), across, 1, 1
    ).reshape(1, -1)
    whole = lax.all_gather(mine, "sub", axis=1, tiled=True)
    block = lax.all_gather(whole, "col", axis=1, tiled=True)
    rows = build_rows(slots, [block], jnp.zeros((1,), jnp.int32))
    columns = lax.all_gather(whole, "row", axis=1, tiled=True)
    start = jnp.zeros((4,), jnp.int32)
    result = correlate(rows, [[columns]], limits, start, factor, None)
    return result.reshape(LAGS, portion, 1, -1)


def solution(mesh):
    return jax.shard_map(
        shards,
        mesh=mesh,
        in_specs=(P("grp", ("row", "col"), "sub"), P(), P("row", None), P()),
        out_specs=P("grp", ("row", "sub"), "col", None),
        check_vma=False,
    )
```

```python
import functools
import math

import jax
import jax.numpy as jnp
from jax import lax
from jax.experimental import pallas as pl
from jax.experimental.pallas import tpu as pltpu
from jax.sharding import PartitionSpec as P

LAGS = 17
PHASES = 8
SLOTS = 128
STABILITY = 1e-05
MESH = pl.DeviceIdType.MESH
VMEM_LIMIT = 8 << 20


def nt_dot(a, b):
    return lax.dot_general(a, b, (((1,), (1,)), ((), ())), preferred_element_type=jnp.float32)


def nn_dot(a, b):
    return jnp.dot(a, b, preferred_element_type=jnp.float32)


def filter_kernel(samples, side_ref, own_ref, other_ref, taps_ref, out_ref, line, filtered):
    margin = 64
    width = own_ref.shape[1]
    window = 3 * 128
    order = lax.broadcasted_iota(jnp.int32, (128, window), 0)
    place = PHASES * (order % 16) + order // 16
    band = jnp.broadcast_to(taps_ref[...], (128, window))
    for bit in range(7):
        moved = pltpu.roll(band, 2 << bit, 1)
        band = jnp.where((place >> bit) & 1 == 1, moved, band)
    band_high = band.astype(jnp.bfloat16)
    band_low = (band - band_high.astype(jnp.float32)).astype(jnp.bfloat16)

    line[...] = jnp.zeros_like(line)

    @pl.when(side_ref[0] == 0)
    def _():
        line[margin : margin + width] = own_ref[0]
        line[margin + width : margin + 2 * width] = other_ref[0]

    @pl.when(side_ref[0] != 0)
    def _():
        line[margin : margin + width] = other_ref[0]
        line[margin + width : margin + 2 * width] = own_ref[0]

    tiles = SLOTS // 16
    row = lax.broadcasted_iota(jnp.int32, (128, 1), 0)
    energy = jnp.zeros((1, line.shape[1]), jnp.float32)
    for tile in range(tiles):
        part = line[256 * tile : 256 * tile + window]
        high = part.astype(jnp.bfloat16)
        low = (part - high.astype(jnp.float32)).astype(jnp.bfloat16)
        value = nn_dot(band_high, high) + (nn_dot(band_high, low) + nn_dot(band_low, high))
        index = PHASES * (16 * tile + row % 16) + row // 16
        value = jnp.where(index < samples, value, 0.0)
        energy = energy + jnp.sum(value * value, axis=0, keepdims=True)
        filtered[tile] = value
    scale = lax.rsqrt(energy / samples + STABILITY)
    for tile in range(tiles):
        value = (filtered[tile] * scale).astype(jnp.bfloat16)
        for phase in range(PHASES):
            out_ref[phase, 0, 16 * tile : 16 * tile + 16, :] = value[16 * phase : 16 * phase + 16]


def whiten(recordings, other, taps, side):
    segments, width, channels = recordings.shape
    half = channels // 2
    block = min(128, half)
    steps = half // block
    samples = width
    own_steps = steps
    if block % 128:
        recordings = lax.dynamic_slice_in_dim(recordings, side[0] * half, half, 2)
        own_steps = 0
    taps_row = jnp.pad(taps.reshape(1, -1), ((0, 0), (0, 384 - taps.shape[0])))
    out = pl.pallas_call(
        functools.partial(filter_kernel, samples),
        out_shape=jax.ShapeDtypeStruct((PHASES, segments, SLOTS, half), jnp.bfloat16),
        grid_spec=pltpu.PrefetchScalarGridSpec(
            num_scalar_prefetch=1,
            grid=(segments, steps),
            in_specs=[
                pl.BlockSpec((1, width, block), lambda s, c, side: (s, 0, side[0] * own_steps + c)),
                pl.BlockSpec((1, width, block), lambda s, c, side: (s, 0, c)),
                pl.BlockSpec((1, 384), lambda s, c, side: (0, 0)),
            ],
            out_specs=pl.BlockSpec((PHASES, 1, SLOTS, block), lambda s, c, side: (0, s, 0, c)),
            scratch_shapes=[
                pltpu.VMEM((256 * (SLOTS // 16 - 1) + 384, block), jnp.float32),
                pltpu.VMEM((SLOTS // 16, 128, block), jnp.float32),
            ],
        ),
        compiler_params=pltpu.CompilerParams(vmem_limit_bytes=16 << 20),
        name="whiten",
    )(side, recordings, other, taps_row)
    return out.reshape(PHASES * segments * SLOTS, half)


def row_blocks():
    blocks = [[(j, 1)] for j in range(PHASES)]

    def minus(a, b):
        return a + [(index, -sign) for index, sign in b]

    def outer(kind, k):
        even, odd, after = [(1 + 2 * k, 1)], [(2 + 2 * k, 1)], [(3 + 2 * k, 1)]
        return [minus(even, odd), odd, minus(after, odd)][kind]

    blocks += [outer(1, k) for k in range(PHASES + 3)]
    for first in (0, 2):
        for second in range(3):
            for k in range(5):
                even, odd = outer(first, 2 * k), outer(first, 2 * k + 1)
                if second == 0:
                    blocks.append(minus(even, odd))
                elif second == 1:
                    blocks.append(odd)
                else:
                    blocks.append(minus(outer(first, 2 * k + 2), odd))
    return blocks


def column_blocks():
    blocks = [[2 * k, 2 * k + 1] for k in range(4)]
    for first in (0, 1):
        for second in ([0], [0, 2], [2]):
            blocks += [[4 * k + first + b for b in second] for k in range(2)]
    return blocks


ROW_BLOCKS = PHASES + PHASES + 3 + 30
COLUMN_BLOCKS = 16


def rows_kernel(count, base_ref, slots_ref, *refs):
    pieces, out_ref, pick, shifted = refs[:count], refs[count], refs[count + 1], refs[count + 2]
    phase = pl.program_id(0)
    rows = slots_ref.shape[0]
    depth = pieces[0].shape[0]

    @pl.when(phase == 0)
    def _():
        first = 0
        for k, piece in enumerate(pieces):
            width = piece.shape[1]
            channel = lax.broadcasted_iota(jnp.int32, (rows, width), 1) + base_ref[k]
            chosen = (slots_ref[...] == channel).astype(jnp.float32).astype(jnp.bfloat16)
            pick[:, first : first + width] = chosen
            first += width

    total = None
    first = 0
    for piece in pieces:
        width = piece.shape[1]
        term = nt_dot(pick[:, first : first + width], piece[...])
        first += width
        total = term if total is None else total + term
    for carry in range(3):
        moved = total
        if carry:
            moved = jnp.concatenate(
                [
                    pltpu.roll(total[:, s : s + SLOTS], carry, 1)
                    for s in range(0, depth, SLOTS)
                ],
                axis=1,
            )
        shifted[(2 - carry) * PHASES + phase] = moved.astype(jnp.bfloat16)

    @pl.when(phase == PHASES - 1)
    def _():
        def block(terms):
            if len(terms) == 1:
                return shifted[terms[0][0]]
            value = None
            for index, sign in terms:
                part = shifted[index].astype(jnp.float32) * sign
                value = part if value is None else value + part
            return value.astype(jnp.bfloat16)

        for slot, terms in enumerate(row_blocks()):
            out_ref[:, slot * depth : (slot + 1) * depth] = block(terms)


def build_rows(slots, pieces, bases):
    rows = slots.shape[0]
    depth = pieces[0].shape[0] // PHASES
    return pl.pallas_call(
        functools.partial(rows_kernel, len(pieces)),
        out_shape=jax.ShapeDtypeStruct((rows, ROW_BLOCKS * depth), jnp.bfloat16),
        grid_spec=pltpu.PrefetchScalarGridSpec(
            num_scalar_prefetch=1,
            grid=(PHASES,),
            in_specs=[pl.BlockSpec((rows, 1), lambda j, base: (0, 0))]
            + [pl.BlockSpec((depth, p.shape[1]), lambda j, base: (j, 0)) for p in pieces],
            out_specs=pl.BlockSpec(
                (rows, ROW_BLOCKS * depth), lambda j, base: (0, 0), pipeline_mode=pl.Buffered(1)
            ),
            scratch_shapes=[
                pltpu.VMEM((rows, sum(p.shape[1] for p in pieces)), jnp.bfloat16),
                pltpu.VMEM((3 * PHASES, rows, depth), jnp.bfloat16),
            ],
        ),
        compiler_params=pltpu.CompilerParams(vmem_limit_bytes=36 << 20),
        name="rows",
    )(bases, slots, *pieces)


def correlate_kernel(factor, count, choices, depth, where_ref, rows_ref, limit_ref, *refs):
    pieces = refs[: count * choices]
    out_ref, held, sums, done = refs[-4:]
    step = pl.program_id(0)
    length = PHASES * depth
    width = held.shape[2]

    @pl.when(step == 0)
    def _():
        for choice in range(choices):

            @pl.when(where_ref[3] == choice)
            def _():
                copies = [
                    pltpu.make_async_copy(pieces[count * choice + k], held.at[k], done.at[k])
                    for k in range(count)
                ]
                for copy in copies:
                    copy.start()
                for copy in copies:
                    copy.wait()

        for k in range(count):
            for slot, phases in enumerate(column_blocks()):
                value = None
                for phase in phases:
                    part = held[k, phase * depth : (phase + 1) * depth].astype(jnp.float32)
                    value = part if value is None else value + part
                sums[k, slot * depth : (slot + 1) * depth] = value.astype(jnp.bfloat16)

    block = min(width, 256)
    for k in range(count):
        for first in range(0, width, block):
            spot = first
            if count > 1:
                spot = pl.multiple_of(where_ref[1 + k] * width + first, block)
            limit = limit_ref[:, pl.ds(spot, block)]

            def write(slot, lag, product, spot=spot, limit=limit):
                value = jnp.where(lag < limit, product, 0.0)
                out_ref[slot, :, pl.ds(spot, block)] = value.astype(jnp.bfloat16)

            @pl.when(step < 4)
            def _():
                quad = 3 - step

                def product(row_slot, column_slot, length):
                    start = pl.multiple_of(row_slot * depth, depth)
                    return factor * nn_dot(
                        rows_ref[:, pl.ds(start, length * depth)],
                        sums[
                            k,
                            column_slot * depth : (column_slot + length) * depth,
                            first : first + block,
                        ],
                    )

                shared = [product(PHASES + 2 * quad + half, 0, 4) for half in range(2)]
                for outer, near in ((0, 0), (1, 1)):

                    def inner(kind):
                        index = 3 * outer + kind
                        return product(2 * PHASES + 3 + 5 * index + quad, 4 + 2 * index, 2)

                    middle = inner(1)
                    for half in range(2):
                        slot = 3 - 2 * half - near
                        write(slot, 4 * step + slot, shared[half] + (middle + inner(2 * half)))

            @pl.when(step == 4)
            def _():
                rows = rows_ref[:, :length]
                write(0, LAGS - 1, factor * nn_dot(rows, held[k, :, first : first + block]))


def correlate(rows, pieces, limits, where, factor, buffer):
    choices, count = len(pieces), len(pieces[0])
    depth = rows.shape[1] // ROW_BLOCKS
    length = PHASES * depth
    portion = rows.shape[0]
    columns = limits.shape[1]
    run = pieces[0][0].shape[1]
    across = count * run
    pieces = [piece for group in pieces for piece in group]
    operands = [where, rows, limits, *pieces]
    in_specs = [
        pl.BlockSpec(rows.shape, lambda l, where: (0, 0), pipeline_mode=pl.Buffered(1)),
        pl.BlockSpec((1, across), lambda l, where: (0, where[0])),
    ] + [pl.BlockSpec(memory_space=pl.ANY) for _ in pieces]
    aliases = {}
    if buffer is not None:
        aliases = {len(operands): 0}
        operands.append(buffer)
        in_specs.append(pl.BlockSpec(memory_space=pl.ANY))
    work = LAGS * portion * across
    return pl.pallas_call(
        functools.partial(correlate_kernel, factor, count, choices, depth),
        out_shape=jax.ShapeDtypeStruct((LAGS, portion, columns), jnp.bfloat16),
        grid_spec=pltpu.PrefetchScalarGridSpec(
            num_scalar_prefetch=1,
            grid=(pl.cdiv(LAGS, 4),),
            in_specs=in_specs,
            out_specs=pl.BlockSpec((4, portion, across), lambda l, where: (l, 0, where[0])),
            scratch_shapes=[
                pltpu.VMEM((count, length, run), jnp.bfloat16),
                pltpu.VMEM((count, COLUMN_BLOCKS * depth, run), jnp.bfloat16),
                pltpu.SemaphoreType.DMA((count,)),
            ],
        ),
        input_output_aliases=aliases,
        compiler_params=pltpu.CompilerParams(vmem_limit_bytes=24 << 20),
        cost_estimate=pl.CostEstimate(
            flops=2 * work * length,
            bytes_accessed=2 * (work + rows.size + length * across),
            transcendentals=0,
        ),
        name="correlate",
    )(*operands)


def whiten_segment(samples, bands, line, store):
    window = 3 * 128
    tiles = SLOTS // 16
    row = lax.broadcasted_iota(jnp.int32, (128, 1), 0)
    energy = jnp.zeros((1, line.shape[1]), jnp.float32)
    for tile in range(tiles):
        part = line[256 * tile : 256 * tile + window]
        high = part.astype(jnp.bfloat16)
        low = (part - high.astype(jnp.float32)).astype(jnp.bfloat16)
        both = nn_dot(bands, high)
        value = both[:128] + (nn_dot(bands[:128], low) + both[128:])
        index = PHASES * (16 * tile + row % 16) + row // 16
        value = jnp.where(index < samples, value, 0.0)
        energy = energy + jnp.sum(value * value, axis=0, keepdims=True)
        line[256 * tile : 256 * tile + 128] = value
    scale = lax.rsqrt(energy / samples + STABILITY)
    for tile in range(tiles):
        value = (line[256 * tile : 256 * tile + 128] * scale).astype(jnp.bfloat16)
        for phase in range(PHASES):
            store(phase, tile, value[16 * phase : 16 * phase + 16])


ORDER = [0, 4, 2, 6, 1, 5, 3, 7]
PLACE = [ORDER.index(phase) for phase in range(PHASES)]
SUMS = [(2 * k, 2 * k + 1) for k in range(4)] + [(0, 2), (4, 6), (1, 3), (5, 7)]


def sum_columns(held, sums):
    depth = sums.shape[0] // len(SUMS)
    for slot, phases in enumerate(SUMS):
        one, two = (held(PLACE[phase], 1).astype(jnp.float32) for phase in phases)
        sums[slot * depth : (slot + 1) * depth] = (one + two).astype(jnp.bfloat16)


def four_lags(rows_ref, held, sums, quad, first, block, write):
    depth = sums.shape[0] // len(SUMS)

    def product(row_slot, columns):
        return nn_dot(rows_ref[:, row_slot * depth : row_slot * depth + columns.shape[0]], columns)

    def summed(slot, length):
        return sums[slot * depth : (slot + length) * depth, first : first + block]

    shared = [product(PHASES + 2 * quad + half, summed(0, 4)) for half in range(2)]
    for outer in range(2):

        def inner(kind):
            if kind == 1:
                columns = summed(4 + 2 * outer, 2)
            else:
                columns = held(4 * outer + kind, 2)[:, first : first + block]
            return product(2 * PHASES + 3 + 5 * (3 * outer + kind) + quad, columns)

        middle = inner(1)
        for half in range(2):
            write(3 - 2 * half - outer, shared[half] + (middle + inner(2 * half)))


def correlate_piece(factor, rows_ref, held, limits, sums, put, after):
    width = sums.shape[1]
    depth = sums.shape[0] // len(SUMS)
    block = 256
    sum_columns(held, sums)

    def masked(product, lag, first):
        value = jnp.where(lag < limits[:, first : first + block], factor * product, 0.0)
        return value.astype(jnp.bfloat16)

    for turn in range(4):
        for first in range(0, width, block):

            def write(index, product, turn=turn, first=first):
                put(turn, index, first, masked(product, 4 * turn + index, first))

            four_lags(rows_ref, held, sums, 3 - turn, first, block, write)
        after(turn)
    for first in range(0, width, block):
        whole = held(0, PHASES)[:, first : first + block]
        product = nn_dot(rows_ref[:, : PHASES * depth], whole)
        put(4, 0, first, masked(product, LAGS - 1, first))
    after(4)


def orders(spot):
    return [
        spot,
        spot - 1 + 2 * ((3 - spot) // 3),
        spot + 1 + (3 - spot) // 3 - 3 * (spot // 3),
        3 * (1 - spot // 2),
    ]


CHUNKS = 4
EARLY = 3


def front_kernel(
    samples, factor,
    raw, taps_in, slots_in, counts_in,
    rows_ref, cols, early_0, early_1, early_2,
    line, band_taps, taps_ref, slots_ref, limit_ref, sums,
    small_sem, own_sem, raw_send, raw_recv, mate_send, mate_recv, x_send, x_recv, xm_send, xm_recv,
    z_send, z_recv,
):
    spot = lax.axis_index("row")
    across = lax.axis_index("col")
    side = lax.axis_index("sub")
    half = line.shape[2]
    channels = 2 * half
    rows = rows_ref.shape[0]
    margin = 64
    width = raw.shape[1]
    mine = pl.ds(pl.multiple_of(side * half, half), half)
    theirs = pl.ds(pl.multiple_of((1 - side) * half, half), half)
    mate = {"sub": 1 - side}
    beside = {"col": 1 - across}
    segments = 2

    place = pl.ds(pl.multiple_of(margin + side * width, 8), width)
    own = [
        pltpu.make_async_copy(raw.at[s, :, mine], line.at[s, place], own_sem.at[s])
        for s in range(segments)
    ]
    for copy in own:
        copy.start()
    small = [
        pltpu.make_async_copy(source, target, small_sem.at[n])
        for n, (source, target) in enumerate(
            [(taps_in, taps_ref), (slots_in, slots_ref), (counts_in, limit_ref)]
        )
    ]
    for copy in small:
        copy.start()

    early = [early_0, early_1, early_2]
    other, pick, shifted = (early_2.at[pl.ds(first, size)] for first, size in ((0, 4), (4, 2), (6, 6)))

    barrier = pltpu.get_barrier_semaphore()
    pl.semaphore_signal(barrier, inc=1, device_id=mate, device_id_type=MESH)
    pl.semaphore_signal(barrier, inc=1, device_id=beside, device_id_type=MESH)

    @pl.when(spot > 0)
    def _():
        pl.semaphore_signal(barrier, inc=1, device_id={"row": spot - 1}, device_id_type=MESH)

    @pl.when(spot < 3)
    def _():
        pl.semaphore_signal(barrier, inc=1, device_id={"row": spot + 1}, device_id_type=MESH)

    pl.semaphore_wait(barrier, 2 + (spot + 2) // 3 + (5 - spot) // 3)

    def remote(source, target, send, recv, device):
        return pltpu.make_async_remote_copy(
            src_ref=source, dst_ref=target, send_sem=send, recv_sem=recv,
            device_id=device, device_id_type=MESH,
        )

    exchange = [
        remote(raw.at[s, :, theirs], line.at[s, place], raw_send.at[s], raw_recv.at[s], mate)
        for s in range(segments)
    ]
    for copy in exchange:
        copy.start()

    def chunk(buffer, k, lanes):
        return buffer.at[pl.ds(4 * (k % 2), 4), k // 2, :, lanes]

    def to_mate(z, k, lanes=mine):
        spotted = chunk(cols.at[z], k, lanes)
        return remote(spotted, spotted, mate_send.at[z, k], mate_recv.at[z, k], mate)

    def to_beside(k):
        return remote(
            chunk(cols.at[spot], k, mine), other.at[k, :, :, mine], x_send.at[k], x_recv.at[k], beside
        )

    def beside_to_mate(k, lanes=mine):
        spotted = other.at[k, :, :, lanes]
        return remote(spotted, spotted, xm_send.at[k], xm_recv.at[k], mate)

    def along(z, k, way):
        spotted = chunk(cols.at[z], k, mine)
        return remote(
            spotted, spotted, z_send.at[way, z, k], z_recv.at[z, k],
            {"row": spot + (1 if way else -1)},
        )

    def poll(distance, k):
        @pl.when(spot >= distance)
        def _():
            z = spot - distance
            along(z, k, 1).wait_recv()
            if distance < 3:

                @pl.when(spot < 3)
                def _():
                    along(z, k, 1).start()

            to_mate(z, k).start()

        @pl.when(spot + distance <= 3)
        def _():
            z = spot + distance
            along(z, k, 0).wait_recv()
            if distance < 3:

                @pl.when(spot > 0)
                def _():
                    along(z, k, 0).start()

            to_mate(z, k).start()

    def settle(distance, k):
        @pl.when(spot >= distance)
        def _():
            z = spot - distance
            if distance < 3:

                @pl.when(spot < 3)
                def _():
                    along(z, k, 1).wait_send()

            to_mate(z, k).wait_send()

        @pl.when(spot + distance <= 3)
        def _():
            z = spot + distance
            if distance < 3:

                @pl.when(spot > 0)
                def _():
                    along(z, k, 0).wait_send()

            to_mate(z, k).wait_send()

    for copy in small:
        copy.wait()

    window = 3 * 128
    band_taps[...] = jnp.zeros_like(band_taps)
    band_taps[:, : taps_ref.shape[1]] = taps_ref[...]
    order = lax.broadcasted_iota(jnp.int32, (128, window), 0)
    shift = PHASES * (order % 16) + order // 16
    band = jnp.broadcast_to(band_taps[...], (128, window))
    for bit in range(7):
        moved = pltpu.roll(band, 2 << bit, 1)
        band = jnp.where((shift >> bit) & 1 == 1, moved, band)
    band_high = band.astype(jnp.bfloat16)
    band_low = (band - band_high.astype(jnp.float32)).astype(jnp.bfloat16)
    bands = jnp.concatenate([band_high, band_low], axis=0)

    end = margin + 2 * width
    for s in range(segments):
        line[s, :margin] = jnp.zeros((margin, half), jnp.float32)
        line[s, end:] = jnp.zeros((line.shape[1] - end, half), jnp.float32)

    slots = slots_ref[:, pl.ds(pl.multiple_of(side * rows, rows), rows)].astype(jnp.float32)
    slots = jnp.broadcast_to(slots, (128, rows)).T
    lane = lax.broadcasted_iota(jnp.int32, (rows, 128), 1)
    for which in range(2):
        first = (across if which == 0 else 1 - across) * channels
        for start in range(0, channels, 128):
            channel = (lane + (first + start)).astype(jnp.float32)
            chosen = (slots == channel).astype(jnp.float32).astype(jnp.bfloat16)
            pick[which, :, :, start : start + 128] = chosen.reshape(4, rows // 4, 128)

    for s in range(segments):
        own[s].wait()
        exchange[s].wait_recv()

        def store(phase, tile, value, s=s):
            cols[spot, PLACE[phase], s, 16 * tile : 16 * tile + 16, mine] = value

        whiten_segment(samples, bands, line.at[s], store)
        for k in (2 * s, 2 * s + 1):
            to_beside(k).start()

            @pl.when(spot > 0)
            def _():
                along(spot, k, 0).start()

            @pl.when(spot < 3)
            def _():
                along(spot, k, 1).start()

            to_mate(spot, k).start()

    depth = segments * SLOTS
    for k in range(CHUNKS):
        s = k // 2
        to_beside(k).wait_recv()
        beside_to_mate(k).start()
        to_mate(spot, k, theirs).wait_recv()
        beside_to_mate(k, theirs).wait_recv()
        for position in range(4 * (k % 2), 4 * (k % 2) + 4):
            phase = ORDER[position]
            total = nt_dot(pick[0].reshape(rows, channels), cols[spot, position, s]) + nt_dot(
                pick[1].reshape(rows, channels), other[k, position % 4]
            )
            for carry in range(3):
                moved = pltpu.roll(total, carry, 1) if carry else total
                at = (2 - carry) * PHASES + phase
                shifted[at // 4, :, :, at % 4 * 128 : at % 4 * 128 + 128] = moved.astype(
                    jnp.bfloat16
                ).reshape(4, rows // 4, 128)
        poll(1, k)
        if k % 2:

            def tile(index, _, s=s):
                at = pl.ds(pl.multiple_of(index * 16, 16), 16)

                def write(slot, value):
                    rows_ref[at, slot * depth + s * SLOTS : slot * depth + (s + 1) * SLOTS] = value

                quarter, inside = index // 8, pl.ds(pl.multiple_of(index % 8 * 16, 16), 16)
                packed = [
                    shifted[i // 4, quarter, inside, i % 4 * 128 : i % 4 * 128 + 128]
                    for i in range(3 * PHASES)
                ]
                plain = [p.astype(jnp.float32) for p in packed]

                def outer(kind, k):
                    even, odd, after = plain[1 + 2 * k], plain[2 + 2 * k], None
                    if kind == 0:
                        return even - odd
                    return plain[3 + 2 * k] - odd

                for j in range(PHASES):
                    write(j, packed[ORDER[j]])
                for j in range(PHASES + 3):
                    write(PHASES + j, packed[2 + 2 * j])
                for number, kind in enumerate((0, 2)):
                    terms = [outer(kind, j) for j in range(PHASES + 3)]
                    at_slot = 2 * PHASES + 3 + 15 * number
                    for j in range(5):
                        odd = terms[2 * j + 1]
                        write(at_slot + j, (terms[2 * j] - odd).astype(jnp.bfloat16))
                        write(at_slot + 5 + j, odd.astype(jnp.bfloat16))
                        write(at_slot + 10 + j, (terms[2 * j + 2] - odd).astype(jnp.bfloat16))
                return 0

            lax.fori_loop(0, rows // 16, tile, 0)

    order_of = orders(spot)
    polls = {
        (0, 1): [(2, 0)], (0, 3): [(2, 1)],
        (1, 1): [(2, 2)], (1, 3): [(2, 3)],
        (2, 0): [(3, 0)], (2, 2): [(3, 1)], (2, 4): [(3, 2), (3, 3)],
    }

    for k in range(CHUNKS):
        beside_to_mate(k).wait_send()

    for index in range(EARLY):
        z = order_of[index]
        if index:
            for k in range(CHUNKS):
                to_mate(z, k, theirs).wait_recv()

        def held(position, count, z=z):
            return cols[z, position : position + count].reshape(count * depth, channels)

        start = pl.multiple_of(z * 2 * channels + across * channels, channels)
        limits = limit_ref[:, pl.ds(start, channels)]

        def put(turn, lag, first, value, index=index):
            size = value.shape[1]
            early[index][4 * turn + lag, :, :, first : first + size] = value.reshape(
                4, rows // 4, size
            )

        def after(turn, index=index):
            for distance, k in polls.get((index, turn), []):
                poll(distance, k)

        correlate_piece(factor, rows_ref, held, limits, sums, put, after)
    for k in range(CHUNKS):
        to_mate(order_of[EARLY], k, theirs).wait_recv()

    for s in range(segments):
        exchange[s].wait_send()
    for k in range(CHUNKS):
        to_beside(k).wait_send()
        to_mate(spot, k).wait_send()

        @pl.when(spot > 0)
        def _():
            along(spot, k, 0).wait_send()

        @pl.when(spot < 3)
        def _():
            along(spot, k, 1).wait_send()

        for distance in (1, 2, 3):
            settle(distance, k)


def front(by_time, taps, slots, counts, factor):
    segments, width, channels = by_time.shape
    half = channels // 2
    rows = slots.shape[1] // 2
    depth = segments * SLOTS
    dma = pltpu.SemaphoreType.DMA
    piece = pltpu.VMEM((LAGS, 4, rows // 4, channels), jnp.bfloat16)
    operands = [pltpu.with_memory_space_constraint(x, pltpu.HBM) for x in (by_time, taps, slots, counts)]
    return pl.pallas_call(
        functools.partial(front_kernel, width, factor),
        out_shape=[
            pltpu.VMEM((rows, ROW_BLOCKS * depth), jnp.bfloat16),
            pltpu.VMEM((4, PHASES, segments, SLOTS, channels), jnp.bfloat16),
            piece, piece, piece,
        ],
        in_specs=[pl.BlockSpec(memory_space=pltpu.HBM)] * 4,
        out_specs=[pl.BlockSpec(memory_space=pltpu.VMEM)] * 5,
        scratch_shapes=[
            pltpu.VMEM((segments, 256 * (SLOTS // 16 - 1) + 384, half), jnp.float32),
            pltpu.VMEM((1, 384), jnp.float32),
            pltpu.VMEM(taps.shape, jnp.float32),
            pltpu.VMEM(slots.shape, jnp.int32),
            pltpu.VMEM(counts.shape, jnp.int32),
            pltpu.VMEM((len(SUMS) * depth, channels), jnp.bfloat16),
            dma((3,)), dma((2,)), dma((2,)), dma((2,)), dma((4, CHUNKS)), dma((4, CHUNKS)),
            dma((CHUNKS,)), dma((CHUNKS,)), dma((CHUNKS,)), dma((CHUNKS,)),
            dma((2, 4, CHUNKS)), dma((4, CHUNKS)),
        ],
        compiler_params=pltpu.CompilerParams(
            vmem_limit_bytes=VMEM_LIMIT, collective_id=0, has_side_effects=True
        ),
        name="front",
    )(*operands)


RING = 10


def back_kernel(
    factor, rows_ref, cols, early_0, early_1, early_2, counts_in, out_ref,
    limit_ref, sums, stage, small_sem, out_sem, early_sem,
):
    spot = lax.axis_index("row")
    across = lax.axis_index("col")
    channels = sums.shape[1]
    rows = rows_ref.shape[0]
    depth = sums.shape[0] // len(SUMS)
    order_of = orders(spot)

    def columns(z):
        return pl.ds(pl.multiple_of(z * channels, channels), channels)

    small = pltpu.make_async_copy(counts_in, limit_ref, small_sem)
    small.start()
    moves = [
        pltpu.make_async_copy(
            early, out_ref.at[:, :, :, columns(order_of[index])], early_sem.at[index]
        )
        for index, early in enumerate((early_0, early_1, early_2))
    ]
    for move in moves:
        move.start()

    z = order_of[3]
    start = pl.multiple_of(z * 2 * channels + across * channels, channels)
    small.wait()
    limits = limit_ref[:, pl.ds(start, channels)]

    def held(position, count):
        return cols[z, position : position + count].reshape(count * depth, channels)

    places = []

    def copy(number):
        lag, first, size = places[number]
        spot_out = pl.ds(pl.multiple_of(z * channels + first, size), size)
        return pltpu.make_async_copy(
            stage.at[number % RING], out_ref.at[lag, :, :, spot_out], out_sem.at[number % RING]
        )

    def put(turn, lag, first, value):
        number, size = len(places), value.shape[1]
        places.append((4 * turn + lag, first, size))
        if number >= RING:
            copy(number - RING).wait()
        stage[number % RING] = value.reshape(4, rows // 4, size)
        copy(number).start()

    correlate_piece(factor, rows_ref, held, limits, sums, put, lambda turn: None)
    for number in range(len(places) - RING, len(places)):
        copy(number).wait()
    for move in moves:
        move.wait()


def back(rows, cols, early, counts, factor):
    portion = rows.shape[0]
    channels = cols.shape[4]
    depth = rows.shape[1] // ROW_BLOCKS
    dma = pltpu.SemaphoreType.DMA
    return pl.pallas_call(
        functools.partial(back_kernel, factor),
        out_shape=jax.ShapeDtypeStruct((LAGS, 4, portion // 4, 4 * channels), jnp.bfloat16),
        in_specs=[pl.BlockSpec(memory_space=pltpu.VMEM)] * 5
        + [pl.BlockSpec(memory_space=pltpu.HBM)],
        out_specs=pl.BlockSpec(memory_space=pltpu.HBM),
        scratch_shapes=[
            pltpu.VMEM(counts.shape, jnp.int32),
            pltpu.VMEM((len(SUMS) * depth, channels), jnp.bfloat16),
            pltpu.VMEM((RING, 4, portion // 4, 256), jnp.bfloat16),
            dma, dma((RING,)), dma((3,)),
        ],
        compiler_params=pltpu.CompilerParams(vmem_limit_bytes=VMEM_LIMIT),
        name="back",
    )(
        *(pltpu.with_memory_space_constraint(x, pltpu.VMEM) for x in (rows, cols, *early)),
        pltpu.with_memory_space_constraint(counts, pltpu.HBM),
    )


def swap(value, axis):
    return lax.ppermute(value, axis, [(0, 1), (1, 0)])


def shards(recordings, filter_taps, slot_table, lag_count):
    segments, channels, width = recordings.shape
    half = channels // 2
    row_count = lax.axis_size("row")
    col_count = lax.axis_size("col")
    portion = slot_table.shape[1] // 2
    factor = 1.0 / math.sqrt(segments * width)
    by_time = recordings.transpose(0, 2, 1)

    if half % 256 == 0 and col_count == 2 and row_count == 4 and portion == channels:
        counts = lag_count.reshape(1, -1)
        taps = filter_taps.reshape(1, -1)
        rows, cols, *early = front(by_time, taps, slot_table, counts, factor)
        result = back(rows, cols, early, counts, factor)
        return result.reshape(LAGS, portion, 1, -1)

    side = lax.axis_index("sub")
    across = lax.axis_index("col")
    away = lax.dynamic_slice_in_dim(by_time, (1 - side) * half, half, 2)
    other = swap(away, "sub")
    mine = whiten(by_time, other, filter_taps, side.reshape(1))
    slots = lax.dynamic_slice_in_dim(slot_table[0], side * portion, portion).reshape(portion, 1)
    limits = lax.dynamic_slice_in_dim(
        lag_count.reshape(row_count, col_count, channels), across, 1, 1
    ).reshape(1, -1)
    whole = lax.all_gather(mine, "sub", axis=1, tiled=True)
    block = lax.all_gather(whole, "col", axis=1, tiled=True)
    rows = build_rows(slots, [block], jnp.zeros((1,), jnp.int32))
    columns = lax.all_gather(whole, "row", axis=1, tiled=True)
    start = jnp.zeros((4,), jnp.int32)
    result = correlate(rows, [[columns]], limits, start, factor, None)
    return result.reshape(LAGS, portion, 1, -1)


def solution(mesh):
    return jax.shard_map(
        shards,
        mesh=mesh,
        in_specs=(P("grp", ("row", "col"), "sub"), P(), P("row", None), P()),
        out_specs=P("grp", ("row", "sub"), "col", None),
        check_vma=False,
    )
```

```python
import functools
import math

import jax
import jax.numpy as jnp
from jax import lax
from jax.experimental import pallas as pl
from jax.experimental.pallas import tpu as pltpu
from jax.sharding import PartitionSpec as P

LAGS = 17
PHASES = 8
SLOTS = 128
STABILITY = 1e-05
MESH = pl.DeviceIdType.MESH
VMEM_LIMIT = 8 << 20


def nt_dot(a, b):
    return lax.dot_general(a, b, (((1,), (1,)), ((), ())), preferred_element_type=jnp.float32)


def nn_dot(a, b):
    return jnp.dot(a, b, preferred_element_type=jnp.float32)


def filter_kernel(samples, side_ref, own_ref, other_ref, taps_ref, out_ref, line, filtered):
    margin = 64
    width = own_ref.shape[1]
    window = 3 * 128
    order = lax.broadcasted_iota(jnp.int32, (128, window), 0)
    place = PHASES * (order % 16) + order // 16
    band = jnp.broadcast_to(taps_ref[...], (128, window))
    for bit in range(7):
        moved = pltpu.roll(band, 2 << bit, 1)
        band = jnp.where((place >> bit) & 1 == 1, moved, band)
    band_high = band.astype(jnp.bfloat16)
    band_low = (band - band_high.astype(jnp.float32)).astype(jnp.bfloat16)

    line[...] = jnp.zeros_like(line)

    @pl.when(side_ref[0] == 0)
    def _():
        line[margin : margin + width] = own_ref[0]
        line[margin + width : margin + 2 * width] = other_ref[0]

    @pl.when(side_ref[0] != 0)
    def _():
        line[margin : margin + width] = other_ref[0]
        line[margin + width : margin + 2 * width] = own_ref[0]

    tiles = SLOTS // 16
    row = lax.broadcasted_iota(jnp.int32, (128, 1), 0)
    energy = jnp.zeros((1, line.shape[1]), jnp.float32)
    for tile in range(tiles):
        part = line[256 * tile : 256 * tile + window]
        high = part.astype(jnp.bfloat16)
        low = (part - high.astype(jnp.float32)).astype(jnp.bfloat16)
        value = nn_dot(band_high, high) + (nn_dot(band_high, low) + nn_dot(band_low, high))
        index = PHASES * (16 * tile + row % 16) + row // 16
        value = jnp.where(index < samples, value, 0.0)
        energy = energy + jnp.sum(value * value, axis=0, keepdims=True)
        filtered[tile] = value
    scale = lax.rsqrt(energy / samples + STABILITY)
    for tile in range(tiles):
        value = (filtered[tile] * scale).astype(jnp.bfloat16)
        for phase in range(PHASES):
            out_ref[phase, 0, 16 * tile : 16 * tile + 16, :] = value[16 * phase : 16 * phase + 16]


def whiten(recordings, other, taps, side):
    segments, width, channels = recordings.shape
    half = channels // 2
    block = min(128, half)
    steps = half // block
    samples = width
    own_steps = steps
    if block % 128:
        recordings = lax.dynamic_slice_in_dim(recordings, side[0] * half, half, 2)
        own_steps = 0
    taps_row = jnp.pad(taps.reshape(1, -1), ((0, 0), (0, 384 - taps.shape[0])))
    out = pl.pallas_call(
        functools.partial(filter_kernel, samples),
        out_shape=jax.ShapeDtypeStruct((PHASES, segments, SLOTS, half), jnp.bfloat16),
        grid_spec=pltpu.PrefetchScalarGridSpec(
            num_scalar_prefetch=1,
            grid=(segments, steps),
            in_specs=[
                pl.BlockSpec((1, width, block), lambda s, c, side: (s, 0, side[0] * own_steps + c)),
                pl.BlockSpec((1, width, block), lambda s, c, side: (s, 0, c)),
                pl.BlockSpec((1, 384), lambda s, c, side: (0, 0)),
            ],
            out_specs=pl.BlockSpec((PHASES, 1, SLOTS, block), lambda s, c, side: (0, s, 0, c)),
            scratch_shapes=[
                pltpu.VMEM((256 * (SLOTS // 16 - 1) + 384, block), jnp.float32),
                pltpu.VMEM((SLOTS // 16, 128, block), jnp.float32),
            ],
        ),
        compiler_params=pltpu.CompilerParams(vmem_limit_bytes=16 << 20),
        name="whiten",
    )(side, recordings, other, taps_row)
    return out.reshape(PHASES * segments * SLOTS, half)


def row_blocks():
    blocks = [[(j, 1)] for j in range(PHASES)]

    def minus(a, b):
        return a + [(index, -sign) for index, sign in b]

    def outer(kind, k):
        even, odd, after = [(1 + 2 * k, 1)], [(2 + 2 * k, 1)], [(3 + 2 * k, 1)]
        return [minus(even, odd), odd, minus(after, odd)][kind]

    blocks += [outer(1, k) for k in range(PHASES + 3)]
    for first in (0, 2):
        for second in range(3):
            for k in range(5):
                even, odd = outer(first, 2 * k), outer(first, 2 * k + 1)
                if second == 0:
                    blocks.append(minus(even, odd))
                elif second == 1:
                    blocks.append(odd)
                else:
                    blocks.append(minus(outer(first, 2 * k + 2), odd))
    return blocks


def column_blocks():
    blocks = [[2 * k, 2 * k + 1] for k in range(4)]
    for first in (0, 1):
        for second in ([0], [0, 2], [2]):
            blocks += [[4 * k + first + b for b in second] for k in range(2)]
    return blocks


ROW_BLOCKS = PHASES + PHASES + 3 + 30
COLUMN_BLOCKS = 16


def rows_kernel(count, base_ref, slots_ref, *refs):
    pieces, out_ref, pick, shifted = refs[:count], refs[count], refs[count + 1], refs[count + 2]
    phase = pl.program_id(0)
    rows = slots_ref.shape[0]
    depth = pieces[0].shape[0]

    @pl.when(phase == 0)
    def _():
        first = 0
        for k, piece in enumerate(pieces):
            width = piece.shape[1]
            channel = lax.broadcasted_iota(jnp.int32, (rows, width), 1) + base_ref[k]
            chosen = (slots_ref[...] == channel).astype(jnp.float32).astype(jnp.bfloat16)
            pick[:, first : first + width] = chosen
            first += width

    total = None
    first = 0
    for piece in pieces:
        width = piece.shape[1]
        term = nt_dot(pick[:, first : first + width], piece[...])
        first += width
        total = term if total is None else total + term
    for carry in range(3):
        moved = total
        if carry:
            moved = jnp.concatenate(
                [
                    pltpu.roll(total[:, s : s + SLOTS], carry, 1)
                    for s in range(0, depth, SLOTS)
                ],
                axis=1,
            )
        shifted[(2 - carry) * PHASES + phase] = moved.astype(jnp.bfloat16)

    @pl.when(phase == PHASES - 1)
    def _():
        def block(terms):
            if len(terms) == 1:
                return shifted[terms[0][0]]
            value = None
            for index, sign in terms:
                part = shifted[index].astype(jnp.float32) * sign
                value = part if value is None else value + part
            return value.astype(jnp.bfloat16)

        for slot, terms in enumerate(row_blocks()):
            out_ref[:, slot * depth : (slot + 1) * depth] = block(terms)


def build_rows(slots, pieces, bases):
    rows = slots.shape[0]
    depth = pieces[0].shape[0] // PHASES
    return pl.pallas_call(
        functools.partial(rows_kernel, len(pieces)),
        out_shape=jax.ShapeDtypeStruct((rows, ROW_BLOCKS * depth), jnp.bfloat16),
        grid_spec=pltpu.PrefetchScalarGridSpec(
            num_scalar_prefetch=1,
            grid=(PHASES,),
            in_specs=[pl.BlockSpec((rows, 1), lambda j, base: (0, 0))]
            + [pl.BlockSpec((depth, p.shape[1]), lambda j, base: (j, 0)) for p in pieces],
            out_specs=pl.BlockSpec(
                (rows, ROW_BLOCKS * depth), lambda j, base: (0, 0), pipeline_mode=pl.Buffered(1)
            ),
            scratch_shapes=[
                pltpu.VMEM((rows, sum(p.shape[1] for p in pieces)), jnp.bfloat16),
                pltpu.VMEM((3 * PHASES, rows, depth), jnp.bfloat16),
            ],
        ),
        compiler_params=pltpu.CompilerParams(vmem_limit_bytes=36 << 20),
        name="rows",
    )(bases, slots, *pieces)


def correlate_kernel(factor, count, choices, depth, where_ref, rows_ref, limit_ref, *refs):
    pieces = refs[: count * choices]
    out_ref, held, sums, done = refs[-4:]
    step = pl.program_id(0)
    length = PHASES * depth
    width = held.shape[2]

    @pl.when(step == 0)
    def _():
        for choice in range(choices):

            @pl.when(where_ref[3] == choice)
            def _():
                copies = [
                    pltpu.make_async_copy(pieces[count * choice + k], held.at[k], done.at[k])
                    for k in range(count)
                ]
                for copy in copies:
                    copy.start()
                for copy in copies:
                    copy.wait()

        for k in range(count):
            for slot, phases in enumerate(column_blocks()):
                value = None
                for phase in phases:
                    part = held[k, phase * depth : (phase + 1) * depth].astype(jnp.float32)
                    value = part if value is None else value + part
                sums[k, slot * depth : (slot + 1) * depth] = value.astype(jnp.bfloat16)

    block = min(width, 256)
    for k in range(count):
        for first in range(0, width, block):
            spot = first
            if count > 1:
                spot = pl.multiple_of(where_ref[1 + k] * width + first, block)
            limit = limit_ref[:, pl.ds(spot, block)]

            def write(slot, lag, product, spot=spot, limit=limit):
                value = jnp.where(lag < limit, product, 0.0)
                out_ref[slot, :, pl.ds(spot, block)] = value.astype(jnp.bfloat16)

            @pl.when(step < 4)
            def _():
                quad = 3 - step

                def product(row_slot, column_slot, length):
                    start = pl.multiple_of(row_slot * depth, depth)
                    return factor * nn_dot(
                        rows_ref[:, pl.ds(start, length * depth)],
                        sums[
                            k,
                            column_slot * depth : (column_slot + length) * depth,
                            first : first + block,
                        ],
                    )

                shared = [product(PHASES + 2 * quad + half, 0, 4) for half in range(2)]
                for outer, near in ((0, 0), (1, 1)):

                    def inner(kind):
                        index = 3 * outer + kind
                        return product(2 * PHASES + 3 + 5 * index + quad, 4 + 2 * index, 2)

                    middle = inner(1)
                    for half in range(2):
                        slot = 3 - 2 * half - near
                        write(slot, 4 * step + slot, shared[half] + (middle + inner(2 * half)))

            @pl.when(step == 4)
            def _():
                rows = rows_ref[:, :length]
                write(0, LAGS - 1, factor * nn_dot(rows, held[k, :, first : first + block]))


def correlate(rows, pieces, limits, where, factor, buffer):
    choices, count = len(pieces), len(pieces[0])
    depth = rows.shape[1] // ROW_BLOCKS
    length = PHASES * depth
    portion = rows.shape[0]
    columns = limits.shape[1]
    run = pieces[0][0].shape[1]
    across = count * run
    pieces = [piece for group in pieces for piece in group]
    operands = [where, rows, limits, *pieces]
    in_specs = [
        pl.BlockSpec(rows.shape, lambda l, where: (0, 0), pipeline_mode=pl.Buffered(1)),
        pl.BlockSpec((1, across), lambda l, where: (0, where[0])),
    ] + [pl.BlockSpec(memory_space=pl.ANY) for _ in pieces]
    aliases = {}
    if buffer is not None:
        aliases = {len(operands): 0}
        operands.append(buffer)
        in_specs.append(pl.BlockSpec(memory_space=pl.ANY))
    work = LAGS * portion * across
    return pl.pallas_call(
        functools.partial(correlate_kernel, factor, count, choices, depth),
        out_shape=jax.ShapeDtypeStruct((LAGS, portion, columns), jnp.bfloat16),
        grid_spec=pltpu.PrefetchScalarGridSpec(
            num_scalar_prefetch=1,
            grid=(pl.cdiv(LAGS, 4),),
            in_specs=in_specs,
            out_specs=pl.BlockSpec((4, portion, across), lambda l, where: (l, 0, where[0])),
            scratch_shapes=[
                pltpu.VMEM((count, length, run), jnp.bfloat16),
                pltpu.VMEM((count, COLUMN_BLOCKS * depth, run), jnp.bfloat16),
                pltpu.SemaphoreType.DMA((count,)),
            ],
        ),
        input_output_aliases=aliases,
        compiler_params=pltpu.CompilerParams(vmem_limit_bytes=24 << 20),
        cost_estimate=pl.CostEstimate(
            flops=2 * work * length,
            bytes_accessed=2 * (work + rows.size + length * across),
            transcendentals=0,
        ),
        name="correlate",
    )(*operands)


def whiten_segment(samples, bands, line, store):
    window = 3 * 128
    tiles = SLOTS // 16
    row = lax.broadcasted_iota(jnp.int32, (128, 1), 0)
    energy = jnp.zeros((1, line.shape[1]), jnp.float32)
    for tile in range(tiles):
        part = line[256 * tile : 256 * tile + window]
        high = part.astype(jnp.bfloat16)
        low = (part - high.astype(jnp.float32)).astype(jnp.bfloat16)
        both = nn_dot(bands, high)
        value = both[:128] + (nn_dot(bands[:128], low) + both[128:])
        index = PHASES * (16 * tile + row % 16) + row // 16
        value = jnp.where(index < samples, value, 0.0)
        energy = energy + jnp.sum(value * value, axis=0, keepdims=True)
        line[256 * tile : 256 * tile + 128] = value
    scale = lax.rsqrt(energy / samples + STABILITY)
    for tile in range(tiles):
        value = (line[256 * tile : 256 * tile + 128] * scale).astype(jnp.bfloat16)
        for phase in range(PHASES):
            store(phase, tile, value[16 * phase : 16 * phase + 16])


ORDER = [0, 4, 2, 6, 1, 5, 3, 7]
PLACE = [ORDER.index(phase) for phase in range(PHASES)]
SUMS = [(2 * k, 2 * k + 1) for k in range(4)] + [(0, 2), (4, 6), (1, 3), (5, 7)]


def sum_columns(held, sums):
    depth = sums.shape[0] // len(SUMS)
    for slot, phases in enumerate(SUMS):
        one, two = (held(PLACE[phase], 1).astype(jnp.float32) for phase in phases)
        sums[slot * depth : (slot + 1) * depth] = (one + two).astype(jnp.bfloat16)


def four_lags(rows_ref, held, sums, quad, first, block, write):
    depth = sums.shape[0] // len(SUMS)

    def product(row_slot, columns):
        return nn_dot(rows_ref[:, row_slot * depth : row_slot * depth + columns.shape[0]], columns)

    def summed(slot, length):
        return sums[slot * depth : (slot + length) * depth, first : first + block]

    shared = [product(PHASES + 2 * quad + half, summed(0, 4)) for half in range(2)]
    for outer in range(2):

        def inner(kind):
            if kind == 1:
                columns = summed(4 + 2 * outer, 2)
            else:
                columns = held(4 * outer + kind, 2)[:, first : first + block]
            return product(2 * PHASES + 3 + 5 * (3 * outer + kind) + quad, columns)

        middle = inner(1)
        for half in range(2):
            write(3 - 2 * half - outer, shared[half] + (middle + inner(2 * half)))


def correlate_piece(factor, rows_ref, held, limits, sums, put, before, after):
    width = sums.shape[1]
    depth = sums.shape[0] // len(SUMS)
    block = 256
    sum_columns(held, sums)

    def masked(product, lag, first):
        value = jnp.where(lag < limits[:, first : first + block], factor * product, 0.0)
        return value.astype(jnp.bfloat16)

    for turn in range(4):
        for first in range(0, width, block):
            before(turn, first)

            def write(index, product, turn=turn, first=first):
                put(turn, index, first, masked(product, 4 * turn + index, first))

            four_lags(rows_ref, held, sums, 3 - turn, first, block, write)
            after(turn, first)
    for first in range(0, width, block):
        before(4, first)
        whole = held(0, PHASES)[:, first : first + block]
        product = nn_dot(rows_ref[:, : PHASES * depth], whole)
        put(4, 0, first, masked(product, LAGS - 1, first))
        after(4, first)


def orders(spot):
    return [
        spot,
        spot - 1 + 2 * ((3 - spot) // 3),
        spot + 1 + (3 - spot) // 3 - 3 * (spot // 3),
        3 * (1 - spot // 2),
    ]


CHUNKS = 4
EARLY = 3


def front_kernel(
    samples, factor,
    raw, taps_in, slots_in, counts_in,
    rows_ref, cols, early_0, early_1, early_2,
    line, band_taps, taps_ref, slots_ref, limit_ref, sums,
    small_sem, own_sem, raw_send, raw_recv, mate_send, mate_recv, x_send, x_recv, xm_send, xm_recv,
    z_send, z_recv,
):
    spot = lax.axis_index("row")
    across = lax.axis_index("col")
    side = lax.axis_index("sub")
    half = line.shape[2]
    channels = 2 * half
    rows = rows_ref.shape[0]
    margin = 64
    width = raw.shape[1]
    mine = pl.ds(pl.multiple_of(side * half, half), half)
    theirs = pl.ds(pl.multiple_of((1 - side) * half, half), half)
    mate = {"sub": 1 - side}
    beside = {"col": 1 - across}
    segments = 2

    place = pl.ds(pl.multiple_of(margin + side * width, 8), width)
    own = [
        pltpu.make_async_copy(raw.at[s, :, mine], line.at[s, place], own_sem.at[s])
        for s in range(segments)
    ]
    for copy in own:
        copy.start()
    small = [
        pltpu.make_async_copy(source, target, small_sem.at[n])
        for n, (source, target) in enumerate(
            [(taps_in, taps_ref), (slots_in, slots_ref), (counts_in, limit_ref)]
        )
    ]
    for copy in small:
        copy.start()

    early = [early_0, early_1, early_2]
    other, pick, shifted = (early_2.at[pl.ds(first, size)] for first, size in ((0, 4), (4, 2), (6, 6)))

    barrier = pltpu.get_barrier_semaphore()
    pl.semaphore_signal(barrier, inc=1, device_id=mate, device_id_type=MESH)
    pl.semaphore_signal(barrier, inc=1, device_id=beside, device_id_type=MESH)

    @pl.when(spot > 0)
    def _():
        pl.semaphore_signal(barrier, inc=1, device_id={"row": spot - 1}, device_id_type=MESH)

    @pl.when(spot < 3)
    def _():
        pl.semaphore_signal(barrier, inc=1, device_id={"row": spot + 1}, device_id_type=MESH)

    pl.semaphore_wait(barrier, 2 + (spot + 2) // 3 + (5 - spot) // 3)

    def remote(source, target, send, recv, device):
        return pltpu.make_async_remote_copy(
            src_ref=source, dst_ref=target, send_sem=send, recv_sem=recv,
            device_id=device, device_id_type=MESH,
        )

    exchange = [
        remote(raw.at[s, :, theirs], line.at[s, place], raw_send.at[s], raw_recv.at[s], mate)
        for s in range(segments)
    ]
    for copy in exchange:
        copy.start()

    def chunk(buffer, k, lanes):
        return buffer.at[pl.ds(4 * (k % 2), 4), k // 2, :, lanes]

    def to_mate(z, k, lanes=mine):
        spotted = chunk(cols.at[z], k, lanes)
        return remote(spotted, spotted, mate_send.at[z, k], mate_recv.at[z, k], mate)

    def to_beside(k):
        return remote(
            chunk(cols.at[spot], k, mine), other.at[k, :, :, mine], x_send.at[k], x_recv.at[k], beside
        )

    def beside_to_mate(k, lanes=mine):
        spotted = other.at[k, :, :, lanes]
        return remote(spotted, spotted, xm_send.at[k], xm_recv.at[k], mate)

    def along(z, k, way):
        spotted = chunk(cols.at[z], k, mine)
        return remote(
            spotted, spotted, z_send.at[way, z, k], z_recv.at[z, k],
            {"row": spot + (1 if way else -1)},
        )

    def poll(distance, k):
        @pl.when(spot >= distance)
        def _():
            z = spot - distance
            along(z, k, 1).wait_recv()
            if distance < 3:

                @pl.when(spot < 3)
                def _():
                    along(z, k, 1).start()

            to_mate(z, k).start()

        @pl.when(spot + distance <= 3)
        def _():
            z = spot + distance
            along(z, k, 0).wait_recv()
            if distance < 3:

                @pl.when(spot > 0)
                def _():
                    along(z, k, 0).start()

            to_mate(z, k).start()

    def settle(distance, k):
        @pl.when(spot >= distance)
        def _():
            z = spot - distance
            if distance < 3:

                @pl.when(spot < 3)
                def _():
                    along(z, k, 1).wait_send()

            to_mate(z, k).wait_send()

        @pl.when(spot + distance <= 3)
        def _():
            z = spot + distance
            if distance < 3:

                @pl.when(spot > 0)
                def _():
                    along(z, k, 0).wait_send()

            to_mate(z, k).wait_send()

    for copy in small:
        copy.wait()

    window = 3 * 128
    band_taps[...] = jnp.zeros_like(band_taps)
    band_taps[:, : taps_ref.shape[1]] = taps_ref[...]
    order = lax.broadcasted_iota(jnp.int32, (128, window), 0)
    shift = PHASES * (order % 16) + order // 16
    band = jnp.broadcast_to(band_taps[...], (128, window))
    for bit in range(7):
        moved = pltpu.roll(band, 2 << bit, 1)
        band = jnp.where((shift >> bit) & 1 == 1, moved, band)
    band_high = band.astype(jnp.bfloat16)
    band_low = (band - band_high.astype(jnp.float32)).astype(jnp.bfloat16)
    bands = jnp.concatenate([band_high, band_low], axis=0)

    end = margin + 2 * width
    for s in range(segments):
        line[s, :margin] = jnp.zeros((margin, half), jnp.float32)
        line[s, end:] = jnp.zeros((line.shape[1] - end, half), jnp.float32)

    slots = slots_ref[:, pl.ds(pl.multiple_of(side * rows, rows), rows)].astype(jnp.float32)
    slots = jnp.broadcast_to(slots, (128, rows)).T
    lane = lax.broadcasted_iota(jnp.int32, (rows, 128), 1)
    for which in range(2):
        first = (across if which == 0 else 1 - across) * channels
        for start in range(0, channels, 128):
            channel = (lane + (first + start)).astype(jnp.float32)
            chosen = (slots == channel).astype(jnp.float32).astype(jnp.bfloat16)
            pick[which, :, :, start : start + 128] = chosen.reshape(4, rows // 4, 128)

    for s in range(segments):
        own[s].wait()
        exchange[s].wait_recv()

        def store(phase, tile, value, s=s):
            cols[spot, PLACE[phase], s, 16 * tile : 16 * tile + 16, mine] = value

        whiten_segment(samples, bands, line.at[s], store)
        for k in (2 * s, 2 * s + 1):
            to_beside(k).start()

            @pl.when(spot > 0)
            def _():
                along(spot, k, 0).start()

            @pl.when(spot < 3)
            def _():
                along(spot, k, 1).start()

            to_mate(spot, k).start()

    depth = segments * SLOTS
    for k in range(CHUNKS):
        s = k // 2
        to_beside(k).wait_recv()
        beside_to_mate(k).start()
        to_mate(spot, k, theirs).wait_recv()
        beside_to_mate(k, theirs).wait_recv()
        for position in range(4 * (k % 2), 4 * (k % 2) + 4):
            phase = ORDER[position]
            total = nt_dot(pick[0].reshape(rows, channels), cols[spot, position, s]) + nt_dot(
                pick[1].reshape(rows, channels), other[k, position % 4]
            )
            for carry in range(3):
                moved = pltpu.roll(total, carry, 1) if carry else total
                at = (2 - carry) * PHASES + phase
                shifted[at // 4, :, :, at % 4 * 128 : at % 4 * 128 + 128] = moved.astype(
                    jnp.bfloat16
                ).reshape(4, rows // 4, 128)
        poll(1, k)
        if k % 2:

            def tile(index, _, s=s):
                at = pl.ds(pl.multiple_of(index * 16, 16), 16)

                def write(slot, value):
                    rows_ref[at, slot * depth + s * SLOTS : slot * depth + (s + 1) * SLOTS] = value

                quarter, inside = index // 8, pl.ds(pl.multiple_of(index % 8 * 16, 16), 16)
                packed = [
                    shifted[i // 4, quarter, inside, i % 4 * 128 : i % 4 * 128 + 128]
                    for i in range(3 * PHASES)
                ]
                plain = [p.astype(jnp.float32) for p in packed]

                def outer(kind, k):
                    even, odd, after = plain[1 + 2 * k], plain[2 + 2 * k], None
                    if kind == 0:
                        return even - odd
                    return plain[3 + 2 * k] - odd

                for j in range(PHASES):
                    write(j, packed[ORDER[j]])
                for j in range(PHASES + 3):
                    write(PHASES + j, packed[2 + 2 * j])
                for number, kind in enumerate((0, 2)):
                    terms = [outer(kind, j) for j in range(PHASES + 3)]
                    at_slot = 2 * PHASES + 3 + 15 * number
                    for j in range(5):
                        odd = terms[2 * j + 1]
                        write(at_slot + j, (terms[2 * j] - odd).astype(jnp.bfloat16))
                        write(at_slot + 5 + j, odd.astype(jnp.bfloat16))
                        write(at_slot + 10 + j, (terms[2 * j + 2] - odd).astype(jnp.bfloat16))
                return 0

            lax.fori_loop(0, rows // 16, tile, 0)

    order_of = orders(spot)
    polls = {
        (0, 1): [(2, 0)], (0, 3): [(2, 1)],
        (1, 1): [(2, 2)], (1, 3): [(2, 3)],
        (2, 0): [(3, 0)], (2, 2): [(3, 1)], (2, 4): [(3, 2), (3, 3)],
    }

    for k in range(CHUNKS):
        beside_to_mate(k).wait_send()

    for index in range(EARLY):
        z = order_of[index]
        if index:
            for k in range(CHUNKS):
                to_mate(z, k, theirs).wait_recv()

        def held(position, count, z=z):
            return cols[z, position : position + count].reshape(count * depth, channels)

        start = pl.multiple_of(z * 2 * channels + across * channels, channels)
        limits = limit_ref[:, pl.ds(start, channels)]

        def put(turn, lag, first, value, index=index):
            size = value.shape[1]
            early[index][4 * turn + lag, :, :, first : first + size] = value.reshape(
                4, rows // 4, size
            )

        def before(turn, first):
            pass

        def after(turn, first, index=index):
            for distance, k in polls.get((index, turn), []) if first else ():
                poll(distance, k)

        correlate_piece(factor, rows_ref, held, limits, sums, put, before, after)
    for k in range(CHUNKS):
        to_mate(order_of[EARLY], k, theirs).wait_recv()

    for s in range(segments):
        exchange[s].wait_send()
    for k in range(CHUNKS):
        to_beside(k).wait_send()
        to_mate(spot, k).wait_send()

        @pl.when(spot > 0)
        def _():
            along(spot, k, 0).wait_send()

        @pl.when(spot < 3)
        def _():
            along(spot, k, 1).wait_send()

        for distance in (1, 2, 3):
            settle(distance, k)


def front(by_time, taps, slots, counts, factor):
    segments, width, channels = by_time.shape
    half = channels // 2
    rows = slots.shape[1] // 2
    depth = segments * SLOTS
    dma = pltpu.SemaphoreType.DMA
    piece = pltpu.VMEM((LAGS, 4, rows // 4, channels), jnp.bfloat16)
    operands = [pltpu.with_memory_space_constraint(x, pltpu.HBM) for x in (by_time, taps, slots, counts)]
    return pl.pallas_call(
        functools.partial(front_kernel, width, factor),
        out_shape=[
            pltpu.VMEM((rows, ROW_BLOCKS * depth), jnp.bfloat16),
            pltpu.VMEM((4, PHASES, segments, SLOTS, channels), jnp.bfloat16),
            piece, piece, piece,
        ],
        in_specs=[pl.BlockSpec(memory_space=pltpu.HBM)] * 4,
        out_specs=[pl.BlockSpec(memory_space=pltpu.VMEM)] * 5,
        scratch_shapes=[
            pltpu.VMEM((segments, 256 * (SLOTS // 16 - 1) + 384, half), jnp.float32),
            pltpu.VMEM((1, 384), jnp.float32),
            pltpu.VMEM(taps.shape, jnp.float32),
            pltpu.VMEM(slots.shape, jnp.int32),
            pltpu.VMEM(counts.shape, jnp.int32),
            pltpu.VMEM((len(SUMS) * depth, channels), jnp.bfloat16),
            dma((3,)), dma((2,)), dma((2,)), dma((2,)), dma((4, CHUNKS)), dma((4, CHUNKS)),
            dma((CHUNKS,)), dma((CHUNKS,)), dma((CHUNKS,)), dma((CHUNKS,)),
            dma((2, 4, CHUNKS)), dma((4, CHUNKS)),
        ],
        compiler_params=pltpu.CompilerParams(
            vmem_limit_bytes=VMEM_LIMIT, collective_id=0, has_side_effects=True
        ),
        name="front",
    )(*operands)


RING = 3
AHEAD = 2
PACE = 2
CUTS = [0, 4, 8, 12, 17]


def back_kernel(
    factor, rows_ref, cols, early_0, early_1, early_2, counts_in, out_ref,
    limit_ref, sums, stage, small_sem, out_sem, early_sem,
):
    spot = lax.axis_index("row")
    across = lax.axis_index("col")
    channels = sums.shape[1]
    rows = rows_ref.shape[0]
    depth = sums.shape[0] // len(SUMS)
    order_of = orders(spot)

    def columns(z):
        return pl.ds(pl.multiple_of(z * channels, channels), channels)

    small = pltpu.make_async_copy(counts_in, limit_ref, small_sem)
    small.start()
    moves = [
        pltpu.make_async_copy(
            early.at[first:last],
            out_ref.at[first:last, :, :, columns(order_of[index])],
            early_sem.at[index, part],
        )
        for part, (first, last) in enumerate(zip(CUTS, CUTS[1:]))
        for index, early in enumerate((early_0, early_1, early_2))
    ]
    started = []

    def advance(count):
        for move in moves[len(started) : len(started) + count]:
            move.start()
            started.append(move)

    advance(AHEAD)

    z = order_of[3]
    start = pl.multiple_of(z * 2 * channels + across * channels, channels)
    small.wait()
    limits = limit_ref[:, pl.ds(start, channels)]

    def held(position, count):
        return cols[z, position : position + count].reshape(count * depth, channels)

    def copies(number):
        turn, first = number // 2, number % 2 * 256
        lags = pl.ds(4 * turn, 1 if turn == 4 else 4)
        lanes = pl.ds(pl.multiple_of(z * channels + first, 256), 256)
        return pltpu.make_async_copy(
            stage.at[number % RING, pl.ds(0, lags.size)],
            out_ref.at[lags, :, :, lanes],
            out_sem.at[number % RING],
        )

    def put(turn, lag, first, value):
        stage[(2 * turn + first // 256) % RING, lag] = value.reshape(4, rows // 4, 256)

    def before(turn, first):
        number = 2 * turn + first // 256
        if number >= RING:
            copies(number - RING).wait()

    def after(turn, first):
        copies(2 * turn + first // 256).start()
        advance(PACE)

    correlate_piece(factor, rows_ref, held, limits, sums, put, before, after)
    for number in range(10 - RING, 10):
        copies(number).wait()
    advance(len(moves))
    for move in moves:
        move.wait()


def back(rows, cols, early, counts, factor):
    portion = rows.shape[0]
    channels = cols.shape[4]
    depth = rows.shape[1] // ROW_BLOCKS
    dma = pltpu.SemaphoreType.DMA
    return pl.pallas_call(
        functools.partial(back_kernel, factor),
        out_shape=jax.ShapeDtypeStruct((LAGS, 4, portion // 4, 4 * channels), jnp.bfloat16),
        in_specs=[pl.BlockSpec(memory_space=pltpu.VMEM)] * 5
        + [pl.BlockSpec(memory_space=pltpu.HBM)],
        out_specs=pl.BlockSpec(memory_space=pltpu.HBM),
        scratch_shapes=[
            pltpu.VMEM(counts.shape, jnp.int32),
            pltpu.VMEM((len(SUMS) * depth, channels), jnp.bfloat16),
            pltpu.VMEM((RING, 4, 4, portion // 4, 256), jnp.bfloat16),
            dma, dma((RING,)), dma((3, len(CUTS) - 1)),
        ],
        compiler_params=pltpu.CompilerParams(vmem_limit_bytes=VMEM_LIMIT),
        name="back",
    )(
        *(pltpu.with_memory_space_constraint(x, pltpu.VMEM) for x in (rows, cols, *early)),
        pltpu.with_memory_space_constraint(counts, pltpu.HBM),
    )


def swap(value, axis):
    return lax.ppermute(value, axis, [(0, 1), (1, 0)])


def shards(recordings, filter_taps, slot_table, lag_count):
    segments, channels, width = recordings.shape
    half = channels // 2
    row_count = lax.axis_size("row")
    col_count = lax.axis_size("col")
    portion = slot_table.shape[1] // 2
    factor = 1.0 / math.sqrt(segments * width)
    by_time = recordings.transpose(0, 2, 1)

    if half % 256 == 0 and col_count == 2 and row_count == 4 and portion == channels:
        counts = lag_count.reshape(1, -1)
        taps = filter_taps.reshape(1, -1)
        rows, cols, *early = front(by_time, taps, slot_table, counts, factor)
        result = back(rows, cols, early, counts, factor)
        return result.reshape(LAGS, portion, 1, -1)

    side = lax.axis_index("sub")
    across = lax.axis_index("col")
    away = lax.dynamic_slice_in_dim(by_time, (1 - side) * half, half, 2)
    other = swap(away, "sub")
    mine = whiten(by_time, other, filter_taps, side.reshape(1))
    slots = lax.dynamic_slice_in_dim(slot_table[0], side * portion, portion).reshape(portion, 1)
    limits = lax.dynamic_slice_in_dim(
        lag_count.reshape(row_count, col_count, channels), across, 1, 1
    ).reshape(1, -1)
    whole = lax.all_gather(mine, "sub", axis=1, tiled=True)
    block = lax.all_gather(whole, "col", axis=1, tiled=True)
    rows = build_rows(slots, [block], jnp.zeros((1,), jnp.int32))
    columns = lax.all_gather(whole, "row", axis=1, tiled=True)
    start = jnp.zeros((4,), jnp.int32)
    result = correlate(rows, [[columns]], limits, start, factor, None)
    return result.reshape(LAGS, portion, 1, -1)


def solution(mesh):
    return jax.shard_map(
        shards,
        mesh=mesh,
        in_specs=(P("grp", ("row", "col"), "sub"), P(), P("row", None), P()),
        out_specs=P("grp", ("row", "sub"), "col", None),
        check_vma=False,
    )
```

```python
import functools
import math

import jax
import jax.numpy as jnp
from jax import lax
from jax.experimental import pallas as pl
from jax.experimental.pallas import tpu as pltpu
from jax.sharding import PartitionSpec as P

LAGS = 17
PHASES = 8
SLOTS = 128
STABILITY = 1e-05
MESH = pl.DeviceIdType.MESH
VMEM_LIMIT = 8 << 20


def nt_dot(a, b):
    return lax.dot_general(a, b, (((1,), (1,)), ((), ())), preferred_element_type=jnp.float32)


def nn_dot(a, b):
    return jnp.dot(a, b, preferred_element_type=jnp.float32)


def filter_kernel(samples, side_ref, own_ref, other_ref, taps_ref, out_ref, line, filtered):
    margin = 64
    width = own_ref.shape[1]
    window = 3 * 128
    order = lax.broadcasted_iota(jnp.int32, (128, window), 0)
    place = PHASES * (order % 16) + order // 16
    band = jnp.broadcast_to(taps_ref[...], (128, window))
    for bit in range(7):
        moved = pltpu.roll(band, 2 << bit, 1)
        band = jnp.where((place >> bit) & 1 == 1, moved, band)
    band_high = band.astype(jnp.bfloat16)
    band_low = (band - band_high.astype(jnp.float32)).astype(jnp.bfloat16)

    line[...] = jnp.zeros_like(line)

    @pl.when(side_ref[0] == 0)
    def _():
        line[margin : margin + width] = own_ref[0]
        line[margin + width : margin + 2 * width] = other_ref[0]

    @pl.when(side_ref[0] != 0)
    def _():
        line[margin : margin + width] = other_ref[0]
        line[margin + width : margin + 2 * width] = own_ref[0]

    tiles = SLOTS // 16
    row = lax.broadcasted_iota(jnp.int32, (128, 1), 0)
    energy = jnp.zeros((1, line.shape[1]), jnp.float32)
    for tile in range(tiles):
        part = line[256 * tile : 256 * tile + window]
        high = part.astype(jnp.bfloat16)
        low = (part - high.astype(jnp.float32)).astype(jnp.bfloat16)
        value = nn_dot(band_high, high) + (nn_dot(band_high, low) + nn_dot(band_low, high))
        index = PHASES * (16 * tile + row % 16) + row // 16
        value = jnp.where(index < samples, value, 0.0)
        energy = energy + jnp.sum(value * value, axis=0, keepdims=True)
        filtered[tile] = value
    scale = lax.rsqrt(energy / samples + STABILITY)
    for tile in range(tiles):
        value = (filtered[tile] * scale).astype(jnp.bfloat16)
        for phase in range(PHASES):
            out_ref[phase, 0, 16 * tile : 16 * tile + 16, :] = value[16 * phase : 16 * phase + 16]


def whiten(recordings, other, taps, side):
    segments, width, channels = recordings.shape
    half = channels // 2
    block = min(128, half)
    steps = half // block
    samples = width
    own_steps = steps
    if block % 128:
        recordings = lax.dynamic_slice_in_dim(recordings, side[0] * half, half, 2)
        own_steps = 0
    taps_row = jnp.pad(taps.reshape(1, -1), ((0, 0), (0, 384 - taps.shape[0])))
    out = pl.pallas_call(
        functools.partial(filter_kernel, samples),
        out_shape=jax.ShapeDtypeStruct((PHASES, segments, SLOTS, half), jnp.bfloat16),
        grid_spec=pltpu.PrefetchScalarGridSpec(
            num_scalar_prefetch=1,
            grid=(segments, steps),
            in_specs=[
                pl.BlockSpec((1, width, block), lambda s, c, side: (s, 0, side[0] * own_steps + c)),
                pl.BlockSpec((1, width, block), lambda s, c, side: (s, 0, c)),
                pl.BlockSpec((1, 384), lambda s, c, side: (0, 0)),
            ],
            out_specs=pl.BlockSpec((PHASES, 1, SLOTS, block), lambda s, c, side: (0, s, 0, c)),
            scratch_shapes=[
                pltpu.VMEM((256 * (SLOTS // 16 - 1) + 384, block), jnp.float32),
                pltpu.VMEM((SLOTS // 16, 128, block), jnp.float32),
            ],
        ),
        compiler_params=pltpu.CompilerParams(vmem_limit_bytes=16 << 20),
        name="whiten",
    )(side, recordings, other, taps_row)
    return out.reshape(PHASES * segments * SLOTS, half)


def row_blocks():
    blocks = [[(j, 1)] for j in range(PHASES)]

    def minus(a, b):
        return a + [(index, -sign) for index, sign in b]

    def outer(kind, k):
        even, odd, after = [(1 + 2 * k, 1)], [(2 + 2 * k, 1)], [(3 + 2 * k, 1)]
        return [minus(even, odd), odd, minus(after, odd)][kind]

    blocks += [outer(1, k) for k in range(PHASES + 3)]
    for first in (0, 2):
        for second in range(3):
            for k in range(5):
                even, odd = outer(first, 2 * k), outer(first, 2 * k + 1)
                if second == 0:
                    blocks.append(minus(even, odd))
                elif second == 1:
                    blocks.append(odd)
                else:
                    blocks.append(minus(outer(first, 2 * k + 2), odd))
    return blocks


def column_blocks():
    blocks = [[2 * k, 2 * k + 1] for k in range(4)]
    for first in (0, 1):
        for second in ([0], [0, 2], [2]):
            blocks += [[4 * k + first + b for b in second] for k in range(2)]
    return blocks


ROW_BLOCKS = PHASES + PHASES + 3 + 30
COLUMN_BLOCKS = 16


def rows_kernel(count, base_ref, slots_ref, *refs):
    pieces, out_ref, pick, shifted = refs[:count], refs[count], refs[count + 1], refs[count + 2]
    phase = pl.program_id(0)
    rows = slots_ref.shape[0]
    depth = pieces[0].shape[0]

    @pl.when(phase == 0)
    def _():
        first = 0
        for k, piece in enumerate(pieces):
            width = piece.shape[1]
            channel = lax.broadcasted_iota(jnp.int32, (rows, width), 1) + base_ref[k]
            chosen = (slots_ref[...] == channel).astype(jnp.float32).astype(jnp.bfloat16)
            pick[:, first : first + width] = chosen
            first += width

    total = None
    first = 0
    for piece in pieces:
        width = piece.shape[1]
        term = nt_dot(pick[:, first : first + width], piece[...])
        first += width
        total = term if total is None else total + term
    for carry in range(3):
        moved = total
        if carry:
            moved = jnp.concatenate(
                [
                    pltpu.roll(total[:, s : s + SLOTS], carry, 1)
                    for s in range(0, depth, SLOTS)
                ],
                axis=1,
            )
        shifted[(2 - carry) * PHASES + phase] = moved.astype(jnp.bfloat16)

    @pl.when(phase == PHASES - 1)
    def _():
        def block(terms):
            if len(terms) == 1:
                return shifted[terms[0][0]]
            value = None
            for index, sign in terms:
                part = shifted[index].astype(jnp.float32) * sign
                value = part if value is None else value + part
            return value.astype(jnp.bfloat16)

        for slot, terms in enumerate(row_blocks()):
            out_ref[:, slot * depth : (slot + 1) * depth] = block(terms)


def build_rows(slots, pieces, bases):
    rows = slots.shape[0]
    depth = pieces[0].shape[0] // PHASES
    return pl.pallas_call(
        functools.partial(rows_kernel, len(pieces)),
        out_shape=jax.ShapeDtypeStruct((rows, ROW_BLOCKS * depth), jnp.bfloat16),
        grid_spec=pltpu.PrefetchScalarGridSpec(
            num_scalar_prefetch=1,
            grid=(PHASES,),
            in_specs=[pl.BlockSpec((rows, 1), lambda j, base: (0, 0))]
            + [pl.BlockSpec((depth, p.shape[1]), lambda j, base: (j, 0)) for p in pieces],
            out_specs=pl.BlockSpec(
                (rows, ROW_BLOCKS * depth), lambda j, base: (0, 0), pipeline_mode=pl.Buffered(1)
            ),
            scratch_shapes=[
                pltpu.VMEM((rows, sum(p.shape[1] for p in pieces)), jnp.bfloat16),
                pltpu.VMEM((3 * PHASES, rows, depth), jnp.bfloat16),
            ],
        ),
        compiler_params=pltpu.CompilerParams(vmem_limit_bytes=36 << 20),
        name="rows",
    )(bases, slots, *pieces)


def correlate_kernel(factor, count, choices, depth, where_ref, rows_ref, limit_ref, *refs):
    pieces = refs[: count * choices]
    out_ref, held, sums, done = refs[-4:]
    step = pl.program_id(0)
    length = PHASES * depth
    width = held.shape[2]

    @pl.when(step == 0)
    def _():
        for choice in range(choices):

            @pl.when(where_ref[3] == choice)
            def _():
                copies = [
                    pltpu.make_async_copy(pieces[count * choice + k], held.at[k], done.at[k])
                    for k in range(count)
                ]
                for copy in copies:
                    copy.start()
                for copy in copies:
                    copy.wait()

        for k in range(count):
            for slot, phases in enumerate(column_blocks()):
                value = None
                for phase in phases:
                    part = held[k, phase * depth : (phase + 1) * depth].astype(jnp.float32)
                    value = part if value is None else value + part
                sums[k, slot * depth : (slot + 1) * depth] = value.astype(jnp.bfloat16)

    block = min(width, 256)
    for k in range(count):
        for first in range(0, width, block):
            spot = first
            if count > 1:
                spot = pl.multiple_of(where_ref[1 + k] * width + first, block)
            limit = limit_ref[:, pl.ds(spot, block)]

            def write(slot, lag, product, spot=spot, limit=limit):
                value = jnp.where(lag < limit, product, 0.0)
                out_ref[slot, :, pl.ds(spot, block)] = value.astype(jnp.bfloat16)

            @pl.when(step < 4)
            def _():
                quad = 3 - step

                def product(row_slot, column_slot, length):
                    start = pl.multiple_of(row_slot * depth, depth)
                    return factor * nn_dot(
                        rows_ref[:, pl.ds(start, length * depth)],
                        sums[
                            k,
                            column_slot * depth : (column_slot + length) * depth,
                            first : first + block,
                        ],
                    )

                shared = [product(PHASES + 2 * quad + half, 0, 4) for half in range(2)]
                for outer, near in ((0, 0), (1, 1)):

                    def inner(kind):
                        index = 3 * outer + kind
                        return product(2 * PHASES + 3 + 5 * index + quad, 4 + 2 * index, 2)

                    middle = inner(1)
                    for half in range(2):
                        slot = 3 - 2 * half - near
                        write(slot, 4 * step + slot, shared[half] + (middle + inner(2 * half)))

            @pl.when(step == 4)
            def _():
                rows = rows_ref[:, :length]
                write(0, LAGS - 1, factor * nn_dot(rows, held[k, :, first : first + block]))


def correlate(rows, pieces, limits, where, factor, buffer):
    choices, count = len(pieces), len(pieces[0])
    depth = rows.shape[1] // ROW_BLOCKS
    length = PHASES * depth
    portion = rows.shape[0]
    columns = limits.shape[1]
    run = pieces[0][0].shape[1]
    across = count * run
    pieces = [piece for group in pieces for piece in group]
    operands = [where, rows, limits, *pieces]
    in_specs = [
        pl.BlockSpec(rows.shape, lambda l, where: (0, 0), pipeline_mode=pl.Buffered(1)),
        pl.BlockSpec((1, across), lambda l, where: (0, where[0])),
    ] + [pl.BlockSpec(memory_space=pl.ANY) for _ in pieces]
    aliases = {}
    if buffer is not None:
        aliases = {len(operands): 0}
        operands.append(buffer)
        in_specs.append(pl.BlockSpec(memory_space=pl.ANY))
    work = LAGS * portion * across
    return pl.pallas_call(
        functools.partial(correlate_kernel, factor, count, choices, depth),
        out_shape=jax.ShapeDtypeStruct((LAGS, portion, columns), jnp.bfloat16),
        grid_spec=pltpu.PrefetchScalarGridSpec(
            num_scalar_prefetch=1,
            grid=(pl.cdiv(LAGS, 4),),
            in_specs=in_specs,
            out_specs=pl.BlockSpec((4, portion, across), lambda l, where: (l, 0, where[0])),
            scratch_shapes=[
                pltpu.VMEM((count, length, run), jnp.bfloat16),
                pltpu.VMEM((count, COLUMN_BLOCKS * depth, run), jnp.bfloat16),
                pltpu.SemaphoreType.DMA((count,)),
            ],
        ),
        input_output_aliases=aliases,
        compiler_params=pltpu.CompilerParams(vmem_limit_bytes=24 << 20),
        cost_estimate=pl.CostEstimate(
            flops=2 * work * length,
            bytes_accessed=2 * (work + rows.size + length * across),
            transcendentals=0,
        ),
        name="correlate",
    )(*operands)


def whiten_segment(samples, bands, line, store, send):
    window = 3 * 128
    tiles = SLOTS // 16
    row = lax.broadcasted_iota(jnp.int32, (128, 1), 0)
    energy = jnp.zeros((1, line.shape[1]), jnp.float32)
    for tile in range(tiles):
        part = line[256 * tile : 256 * tile + window]
        high = part.astype(jnp.bfloat16)
        low = (part - high.astype(jnp.float32)).astype(jnp.bfloat16)
        both = nn_dot(bands, high)
        value = both[:128] + (nn_dot(bands[:128], low) + both[128:])
        index = PHASES * (16 * tile + row % 16) + row // 16
        value = jnp.where(index < samples, value, 0.0)
        energy = energy + jnp.sum(value * value, axis=0, keepdims=True)
        line[256 * tile : 256 * tile + 128] = value
    scale = lax.rsqrt(energy / samples + STABILITY)
    for part in range(2):
        for tile in range(tiles):
            for phase in ORDER[4 * part : 4 * part + 4]:
                first = 256 * tile + 16 * phase
                store(phase, tile, (line[first : first + 16] * scale).astype(jnp.bfloat16))
        send(part)


ORDER = [0, 4, 2, 6, 1, 5, 3, 7]
PLACE = [ORDER.index(phase) for phase in range(PHASES)]
SUMS = [(2 * k, 2 * k + 1) for k in range(4)] + [(0, 2), (4, 6), (1, 3), (5, 7)]


def sum_columns(held, sums):
    depth = sums.shape[0] // len(SUMS)
    for slot, phases in enumerate(SUMS):
        one, two = (held(PLACE[phase], 1).astype(jnp.float32) for phase in phases)
        sums[slot * depth : (slot + 1) * depth] = (one + two).astype(jnp.bfloat16)


def four_lags(rows_ref, held, sums, quad, first, block, write):
    depth = sums.shape[0] // len(SUMS)

    def product(row_slot, columns):
        return nn_dot(rows_ref[:, row_slot * depth : row_slot * depth + columns.shape[0]], columns)

    def summed(slot, length):
        return sums[slot * depth : (slot + length) * depth, first : first + block]

    shared = [product(PHASES + 2 * quad + half, summed(0, 4)) for half in range(2)]
    for outer in range(2):

        def inner(kind):
            if kind == 1:
                columns = summed(4 + 2 * outer, 2)
            else:
                columns = held(4 * outer + kind, 2)[:, first : first + block]
            return product(2 * PHASES + 3 + 5 * (3 * outer + kind) + quad, columns)

        middle = inner(1)
        for half in range(2):
            write(3 - 2 * half - outer, shared[half] + (middle + inner(2 * half)))


def correlate_piece(factor, rows_ref, held, limits, sums, put, before, after):
    width = sums.shape[1]
    depth = sums.shape[0] // len(SUMS)
    block = 256
    sum_columns(held, sums)

    def masked(product, lag, first):
        value = jnp.where(lag < limits[:, first : first + block], factor * product, 0.0)
        return value.astype(jnp.bfloat16)

    for turn in range(4):
        for first in range(0, width, block):
            before(turn, first)

            def write(index, product, turn=turn, first=first):
                put(turn, index, first, masked(product, 4 * turn + index, first))

            four_lags(rows_ref, held, sums, 3 - turn, first, block, write)
            after(turn, first)
    for first in range(0, width, block):
        before(4, first)
        whole = held(0, PHASES)[:, first : first + block]
        product = nn_dot(rows_ref[:, : PHASES * depth], whole)
        put(4, 0, first, masked(product, LAGS - 1, first))
        after(4, first)


def orders(spot):
    return [
        spot,
        spot - 1 + 2 * ((3 - spot) // 3),
        spot + 1 + (3 - spot) // 3 - 3 * (spot // 3),
        3 * (1 - spot // 2),
    ]


CHUNKS = 4
EARLY = 3


def front_kernel(
    samples, factor,
    raw, taps_in, slots_in, counts_in,
    rows_ref, cols, early_0, early_1, early_2,
    line, band_taps, taps_ref, slots_ref, limit_ref, sums,
    small_sem, own_sem, raw_send, raw_recv, mate_send, mate_recv, x_send, x_recv, xm_send, xm_recv,
    z_send, z_recv,
):
    spot = lax.axis_index("row")
    across = lax.axis_index("col")
    side = lax.axis_index("sub")
    half = line.shape[2]
    channels = 2 * half
    rows = rows_ref.shape[0]
    margin = 64
    width = raw.shape[1]
    mine = pl.ds(pl.multiple_of(side * half, half), half)
    theirs = pl.ds(pl.multiple_of((1 - side) * half, half), half)
    mate = {"sub": 1 - side}
    beside = {"col": 1 - across}
    segments = 2

    place = pl.ds(pl.multiple_of(margin + side * width, 8), width)
    own = [
        pltpu.make_async_copy(raw.at[s, :, mine], line.at[s, place], own_sem.at[s])
        for s in range(segments)
    ]
    for copy in own:
        copy.start()
    small = [
        pltpu.make_async_copy(source, target, small_sem.at[n])
        for n, (source, target) in enumerate(
            [(taps_in, taps_ref), (slots_in, slots_ref), (counts_in, limit_ref)]
        )
    ]
    for copy in small:
        copy.start()

    early = [early_0, early_1, early_2]
    other, pick, shifted = (early_2.at[pl.ds(first, size)] for first, size in ((0, 4), (4, 2), (6, 6)))

    barrier = pltpu.get_barrier_semaphore()
    pl.semaphore_signal(barrier, inc=1, device_id=mate, device_id_type=MESH)
    pl.semaphore_signal(barrier, inc=1, device_id=beside, device_id_type=MESH)

    @pl.when(spot > 0)
    def _():
        pl.semaphore_signal(barrier, inc=1, device_id={"row": spot - 1}, device_id_type=MESH)

    @pl.when(spot < 3)
    def _():
        pl.semaphore_signal(barrier, inc=1, device_id={"row": spot + 1}, device_id_type=MESH)

    pl.semaphore_wait(barrier, 2 + (spot + 2) // 3 + (5 - spot) // 3)

    def remote(source, target, send, recv, device):
        return pltpu.make_async_remote_copy(
            src_ref=source, dst_ref=target, send_sem=send, recv_sem=recv,
            device_id=device, device_id_type=MESH,
        )

    exchange = [
        remote(raw.at[s, :, theirs], line.at[s, place], raw_send.at[s], raw_recv.at[s], mate)
        for s in range(segments)
    ]
    for copy in exchange:
        copy.start()

    def chunk(buffer, k, lanes):
        return buffer.at[pl.ds(4 * (k % 2), 4), k // 2, :, lanes]

    def to_mate(z, k, lanes=mine):
        spotted = chunk(cols.at[z], k, lanes)
        return remote(spotted, spotted, mate_send.at[z, k], mate_recv.at[z, k], mate)

    def to_beside(k):
        return remote(
            chunk(cols.at[spot], k, mine), other.at[k, :, :, mine], x_send.at[k], x_recv.at[k], beside
        )

    def beside_to_mate(k, lanes=mine):
        spotted = other.at[k, :, :, lanes]
        return remote(spotted, spotted, xm_send.at[k], xm_recv.at[k], mate)

    def along(z, k, way):
        spotted = chunk(cols.at[z], k, mine)
        return remote(
            spotted, spotted, z_send.at[way, z, k], z_recv.at[z, k],
            {"row": spot + (1 if way else -1)},
        )

    def poll(distance, k):
        @pl.when(spot >= distance)
        def _():
            z = spot - distance
            along(z, k, 1).wait_recv()
            if distance < 3:

                @pl.when(spot < 3)
                def _():
                    along(z, k, 1).start()

            to_mate(z, k).start()

        @pl.when(spot + distance <= 3)
        def _():
            z = spot + distance
            along(z, k, 0).wait_recv()
            if distance < 3:

                @pl.when(spot > 0)
                def _():
                    along(z, k, 0).start()

            to_mate(z, k).start()

    def settle(distance, k):
        @pl.when(spot >= distance)
        def _():
            z = spot - distance
            if distance < 3:

                @pl.when(spot < 3)
                def _():
                    along(z, k, 1).wait_send()

            to_mate(z, k).wait_send()

        @pl.when(spot + distance <= 3)
        def _():
            z = spot + distance
            if distance < 3:

                @pl.when(spot > 0)
                def _():
                    along(z, k, 0).wait_send()

            to_mate(z, k).wait_send()

    for copy in small:
        copy.wait()

    window = 3 * 128
    band_taps[...] = jnp.zeros_like(band_taps)
    band_taps[:, : taps_ref.shape[1]] = taps_ref[...]
    order = lax.broadcasted_iota(jnp.int32, (128, window), 0)
    shift = PHASES * (order % 16) + order // 16
    band = jnp.broadcast_to(band_taps[...], (128, window))
    for bit in range(7):
        moved = pltpu.roll(band, 2 << bit, 1)
        band = jnp.where((shift >> bit) & 1 == 1, moved, band)
    band_high = band.astype(jnp.bfloat16)
    band_low = (band - band_high.astype(jnp.float32)).astype(jnp.bfloat16)
    bands = jnp.concatenate([band_high, band_low], axis=0)

    end = margin + 2 * width
    for s in range(segments):
        line[s, :margin] = jnp.zeros((margin, half), jnp.float32)
        line[s, end:] = jnp.zeros((line.shape[1] - end, half), jnp.float32)

    slots = slots_ref[:, pl.ds(pl.multiple_of(side * rows, rows), rows)].astype(jnp.float32)
    slots = jnp.broadcast_to(slots, (128, rows)).T
    lane = lax.broadcasted_iota(jnp.int32, (rows, 128), 1)
    for which in range(2):
        first = (across if which == 0 else 1 - across) * channels
        for start in range(0, channels, 128):
            channel = (lane + (first + start)).astype(jnp.float32)
            chosen = (slots == channel).astype(jnp.float32).astype(jnp.bfloat16)
            pick[which, :, :, start : start + 128] = chosen.reshape(4, rows // 4, 128)

    for s in range(segments):
        own[s].wait()
        exchange[s].wait_recv()

        def store(phase, tile, value, s=s):
            cols[spot, PLACE[phase], s, 16 * tile : 16 * tile + 16, mine] = value

        def send(part, s=s):
            k = 2 * s + part

            @pl.when(spot > 0)
            def _():
                along(spot, k, 0).start()

            @pl.when(spot < 3)
            def _():
                along(spot, k, 1).start()

            to_beside(k).start()
            to_mate(spot, k).start()

        whiten_segment(samples, bands, line.at[s], store, send)

    depth = segments * SLOTS
    for k in range(CHUNKS):
        s = k // 2
        to_beside(k).wait_recv()
        beside_to_mate(k).start()
        to_mate(spot, k, theirs).wait_recv()
        beside_to_mate(k, theirs).wait_recv()
        for position in range(4 * (k % 2), 4 * (k % 2) + 4):
            phase = ORDER[position]
            total = nt_dot(pick[0].reshape(rows, channels), cols[spot, position, s]) + nt_dot(
                pick[1].reshape(rows, channels), other[k, position % 4]
            )
            for carry in range(3):
                moved = pltpu.roll(total, carry, 1) if carry else total
                at = (2 - carry) * PHASES + phase
                shifted[at // 4, :, :, at % 4 * 128 : at % 4 * 128 + 128] = moved.astype(
                    jnp.bfloat16
                ).reshape(4, rows // 4, 128)
        poll(1, k)
        if k % 2:

            def tile(index, _, s=s):
                at = pl.ds(pl.multiple_of(index * 16, 16), 16)

                def write(slot, value):
                    rows_ref[at, slot * depth + s * SLOTS : slot * depth + (s + 1) * SLOTS] = value

                quarter, inside = index // 8, pl.ds(pl.multiple_of(index % 8 * 16, 16), 16)
                packed = [
                    shifted[i // 4, quarter, inside, i % 4 * 128 : i % 4 * 128 + 128]
                    for i in range(3 * PHASES)
                ]
                plain = [p.astype(jnp.float32) for p in packed]

                def outer(kind, k):
                    even, odd, after = plain[1 + 2 * k], plain[2 + 2 * k], None
                    if kind == 0:
                        return even - odd
                    return plain[3 + 2 * k] - odd

                for j in range(PHASES):
                    write(j, packed[ORDER[j]])
                for j in range(PHASES + 3):
                    write(PHASES + j, packed[2 + 2 * j])
                for number, kind in enumerate((0, 2)):
                    terms = [outer(kind, j) for j in range(PHASES + 3)]
                    at_slot = 2 * PHASES + 3 + 15 * number
                    for j in range(5):
                        odd = terms[2 * j + 1]
                        write(at_slot + j, (terms[2 * j] - odd).astype(jnp.bfloat16))
                        write(at_slot + 5 + j, odd.astype(jnp.bfloat16))
                        write(at_slot + 10 + j, (terms[2 * j + 2] - odd).astype(jnp.bfloat16))
                return 0

            lax.fori_loop(0, rows // 16, tile, 0)

    order_of = orders(spot)
    polls = {
        (0, 1): [(2, 0)], (0, 3): [(2, 1)],
        (1, 1): [(2, 2)], (1, 3): [(2, 3)],
        (2, 0): [(3, 0)], (2, 2): [(3, 1)], (2, 4): [(3, 2), (3, 3)],
    }

    for k in range(CHUNKS):
        beside_to_mate(k).wait_send()

    for index in range(EARLY):
        z = order_of[index]
        if index:
            for k in range(CHUNKS):
                to_mate(z, k, theirs).wait_recv()

        def held(position, count, z=z):
            return cols[z, position : position + count].reshape(count * depth, channels)

        start = pl.multiple_of(z * 2 * channels + across * channels, channels)
        limits = limit_ref[:, pl.ds(start, channels)]

        def put(turn, lag, first, value, index=index):
            size = value.shape[1]
            early[index][4 * turn + lag, :, :, first : first + size] = value.reshape(
                4, rows // 4, size
            )

        def before(turn, first):
            pass

        def after(turn, first, index=index):
            for distance, k in polls.get((index, turn), []) if first else ():
                poll(distance, k)

        correlate_piece(factor, rows_ref, held, limits, sums, put, before, after)
    for k in range(CHUNKS):
        to_mate(order_of[EARLY], k, theirs).wait_recv()

    for s in range(segments):
        exchange[s].wait_send()
    for k in range(CHUNKS):
        to_beside(k).wait_send()
        to_mate(spot, k).wait_send()

        @pl.when(spot > 0)
        def _():
            along(spot, k, 0).wait_send()

        @pl.when(spot < 3)
        def _():
            along(spot, k, 1).wait_send()

        for distance in (1, 2, 3):
            settle(distance, k)


def front(by_time, taps, slots, counts, factor):
    segments, width, channels = by_time.shape
    half = channels // 2
    rows = slots.shape[1] // 2
    depth = segments * SLOTS
    dma = pltpu.SemaphoreType.DMA
    piece = pltpu.VMEM((LAGS, 4, rows // 4, channels), jnp.bfloat16)
    operands = [pltpu.with_memory_space_constraint(x, pltpu.HBM) for x in (by_time, taps, slots, counts)]
    return pl.pallas_call(
        functools.partial(front_kernel, width, factor),
        out_shape=[
            pltpu.VMEM((rows, ROW_BLOCKS * depth), jnp.bfloat16),
            pltpu.VMEM((4, PHASES, segments, SLOTS, channels), jnp.bfloat16),
            piece, piece, piece,
        ],
        in_specs=[pl.BlockSpec(memory_space=pltpu.HBM)] * 4,
        out_specs=[pl.BlockSpec(memory_space=pltpu.VMEM)] * 5,
        scratch_shapes=[
            pltpu.VMEM((segments, 256 * (SLOTS // 16 - 1) + 384, half), jnp.float32),
            pltpu.VMEM((1, 384), jnp.float32),
            pltpu.VMEM(taps.shape, jnp.float32),
            pltpu.VMEM(slots.shape, jnp.int32),
            pltpu.VMEM(counts.shape, jnp.int32),
            pltpu.VMEM((len(SUMS) * depth, channels), jnp.bfloat16),
            dma((3,)), dma((2,)), dma((2,)), dma((2,)), dma((4, CHUNKS)), dma((4, CHUNKS)),
            dma((CHUNKS,)), dma((CHUNKS,)), dma((CHUNKS,)), dma((CHUNKS,)),
            dma((2, 4, CHUNKS)), dma((4, CHUNKS)),
        ],
        compiler_params=pltpu.CompilerParams(
            vmem_limit_bytes=VMEM_LIMIT, collective_id=0, has_side_effects=True
        ),
        name="front",
    )(*operands)


RING = 3
AHEAD = 2
PACE = 2
CUTS = [0, 4, 8, 12, 17]


def back_kernel(
    factor, rows_ref, cols, early_0, early_1, early_2, counts_in, out_ref,
    limit_ref, sums, stage, small_sem, out_sem, early_sem,
):
    spot = lax.axis_index("row")
    across = lax.axis_index("col")
    channels = sums.shape[1]
    rows = rows_ref.shape[0]
    depth = sums.shape[0] // len(SUMS)
    order_of = orders(spot)

    def columns(z):
        return pl.ds(pl.multiple_of(z * channels, channels), channels)

    small = pltpu.make_async_copy(counts_in, limit_ref, small_sem)
    small.start()
    moves = [
        pltpu.make_async_copy(
            early.at[first:last],
            out_ref.at[first:last, :, :, columns(order_of[index])],
            early_sem.at[index, part],
        )
        for part, (first, last) in enumerate(zip(CUTS, CUTS[1:]))
        for index, early in enumerate((early_0, early_1, early_2))
    ]
    started = []

    def advance(count):
        for move in moves[len(started) : len(started) + count]:
            move.start()
            started.append(move)

    advance(AHEAD)

    z = order_of[3]
    start = pl.multiple_of(z * 2 * channels + across * channels, channels)
    small.wait()
    limits = limit_ref[:, pl.ds(start, channels)]

    def held(position, count):
        return cols[z, position : position + count].reshape(count * depth, channels)

    def copies(number):
        turn, first = number // 2, number % 2 * 256
        lags = pl.ds(4 * turn, 1 if turn == 4 else 4)
        lanes = pl.ds(pl.multiple_of(z * channels + first, 256), 256)
        return pltpu.make_async_copy(
            stage.at[number % RING, pl.ds(0, lags.size)],
            out_ref.at[lags, :, :, lanes],
            out_sem.at[number % RING],
        )

    def put(turn, lag, first, value):
        stage[(2 * turn + first // 256) % RING, lag] = value.reshape(4, rows // 4, 256)

    def before(turn, first):
        number = 2 * turn + first // 256
        if number >= RING:
            copies(number - RING).wait()

    def after(turn, first):
        copies(2 * turn + first // 256).start()
        advance(PACE)

    correlate_piece(factor, rows_ref, held, limits, sums, put, before, after)
    for number in range(10 - RING, 10):
        copies(number).wait()
    advance(len(moves))
    for move in moves:
        move.wait()


def back(rows, cols, early, counts, factor):
    portion = rows.shape[0]
    channels = cols.shape[4]
    depth = rows.shape[1] // ROW_BLOCKS
    dma = pltpu.SemaphoreType.DMA
    return pl.pallas_call(
        functools.partial(back_kernel, factor),
        out_shape=jax.ShapeDtypeStruct((LAGS, 4, portion // 4, 4 * channels), jnp.bfloat16),
        in_specs=[pl.BlockSpec(memory_space=pltpu.VMEM)] * 5
        + [pl.BlockSpec(memory_space=pltpu.HBM)],
        out_specs=pl.BlockSpec(memory_space=pltpu.HBM),
        scratch_shapes=[
            pltpu.VMEM(counts.shape, jnp.int32),
            pltpu.VMEM((len(SUMS) * depth, channels), jnp.bfloat16),
            pltpu.VMEM((RING, 4, 4, portion // 4, 256), jnp.bfloat16),
            dma, dma((RING,)), dma((3, len(CUTS) - 1)),
        ],
        compiler_params=pltpu.CompilerParams(vmem_limit_bytes=VMEM_LIMIT),
        name="back",
    )(
        *(pltpu.with_memory_space_constraint(x, pltpu.VMEM) for x in (rows, cols, *early)),
        pltpu.with_memory_space_constraint(counts, pltpu.HBM),
    )


def swap(value, axis):
    return lax.ppermute(value, axis, [(0, 1), (1, 0)])


def shards(recordings, filter_taps, slot_table, lag_count):
    segments, channels, width = recordings.shape
    half = channels // 2
    row_count = lax.axis_size("row")
    col_count = lax.axis_size("col")
    portion = slot_table.shape[1] // 2
    factor = 1.0 / math.sqrt(segments * width)
    by_time = recordings.transpose(0, 2, 1)

    if half % 256 == 0 and col_count == 2 and row_count == 4 and portion == channels:
        counts = lag_count.reshape(1, -1)
        taps = filter_taps.reshape(1, -1)
        rows, cols, *early = front(by_time, taps, slot_table, counts, factor)
        result = back(rows, cols, early, counts, factor)
        return result.reshape(LAGS, portion, 1, -1)

    side = lax.axis_index("sub")
    across = lax.axis_index("col")
    away = lax.dynamic_slice_in_dim(by_time, (1 - side) * half, half, 2)
    other = swap(away, "sub")
    mine = whiten(by_time, other, filter_taps, side.reshape(1))
    slots = lax.dynamic_slice_in_dim(slot_table[0], side * portion, portion).reshape(portion, 1)
    limits = lax.dynamic_slice_in_dim(
        lag_count.reshape(row_count, col_count, channels), across, 1, 1
    ).reshape(1, -1)
    whole = lax.all_gather(mine, "sub", axis=1, tiled=True)
    block = lax.all_gather(whole, "col", axis=1, tiled=True)
    rows = build_rows(slots, [block], jnp.zeros((1,), jnp.int32))
    columns = lax.all_gather(whole, "row", axis=1, tiled=True)
    start = jnp.zeros((4,), jnp.int32)
    result = correlate(rows, [[columns]], limits, start, factor, None)
    return result.reshape(LAGS, portion, 1, -1)


def solution(mesh):
    return jax.shard_map(
        shards,
        mesh=mesh,
        in_specs=(P("grp", ("row", "col"), "sub"), P(), P("row", None), P()),
        out_specs=P("grp", ("row", "sub"), "col", None),
        check_vma=False,
    )
```
